512 devices in a mesh: leaf: 32 (over z, core), front: 16 (over y, x).
Axes of the slice: x: 4, y: 4, z: 16, core: 2. Of those that a mesh axis runs over, the one named last changes fastest.
Arguments:
- forcing: bfloat16 [32, 10240, 128], P('leaf', 'front'), may hold values from -6 to 6
- live: int32 [2, 32], replicated, may hold values from 40 to 80, as said below
- lower_inv: bfloat16 [32, 10240, 960], P('leaf', 'front'), may hold values from -0.0625 to 0.0625
- lower_upd: bfloat16 [32, 10240, 640], P('leaf', 'front'), may hold values from -0.0625 to 0.0625
- upper_inv: bfloat16 [32, 10240, 960], P('leaf', 'front'), may hold values from -0.0625 to 0.0625
- upper_upd: bfloat16 [32, 10240, 640], P('leaf', 'front'), may hold values from -0.0625 to 0.0625
Outputs:
- solution: bfloat16 [2, 32, 10240, 128], P(None, 'leaf', 'front')
The draws below stay inside these ranges and needn't reach their ends.
Inputs may be any that keep to these rules, and one draw needn't show every extreme that they name: Entries (l, j) with j at or beyond 2**(1 - l) are not read. The root's separator is live in full.
All inputs are finite; a program needn't handle non-finite values.
Results may differ from the reference program's by a relative error of at most 0.008.
Values may be sent and summed in bfloat16 or wider, within the bound.
No kernel may reach another device: no remote copies, remote signals or barrier semaphores. Data moves between devices by JAX's collectives and lax.ppermute only.
A program may use at most 64 MiB of HBM per device.

```python
import jax
import jax.numpy as jnp

NRHS = 128
SEP = 10240
BLK = 128
LEV = 2
LEAVES = 32
NBLK = 80
COLS = 960
GCOLS = 640


def draw_live(key, part):
    counts = jax.random.randint(key, (LEV, LEAVES), NBLK // 2, NBLK + 1)
    fullest = jax.random.randint(jax.random.fold_in(key, 7), (), 0, 2 ** (LEV - 1))
    row = jnp.arange(LEV)[:, None]
    column = jnp.arange(LEAVES)[None, :]
    counts = jnp.where((row == 0) & (column == fullest), NBLK, counts)
    counts = jnp.where((row == LEV - 1) & (column == 0), NBLK, counts)
    counts = jnp.where((row == LEV - 1) & (column == LEAVES - 1), NBLK // 2, counts)
    return counts.astype(jnp.int32)


def block_scale(key, dims, split, least, top_value):
    def one(position, shards_of):
        steps = jax.random.uniform(jax.random.fold_in(jax.random.fold_in(key, 6), position), (shards_of,), jnp.float32, least / len(split), top_value / len(split))
        return jnp.repeat(jnp.exp(steps), dims[position] // shards_of).reshape((-1,) + (1,) * (len(dims) - position - 1))

    factor_of = one(*split[0])
    for cut in split[1:]:
        factor_of = factor_of * one(*cut)
    return factor_of


def normal_values(stream_key, dims, scale, most, shards=(), dtype=jnp.bfloat16):
    entries = jax.random.normal(stream_key, dims, jnp.float32) * scale
    if len(shards) > 0:
        entries = block_scale(stream_key, dims, shards, -0.22, 0.18) * entries
    return jnp.clip(entries, min=-most, max=most).astype(dtype)


def setup_inputs(seed: int = 0) -> dict:
    keys = jax.random.split(jax.random.key(seed), 7)
    forcing = normal_values(keys[0], (LEAVES, SEP, NRHS), 1.0, 6.0, ((0, 32), (1, 16)))
    live = draw_live(jax.random.fold_in(keys[6], 71), 0)
    lower_inv = normal_values(keys[2], (LEAVES, SEP, COLS), SEP ** -0.5, 0.0625, ((0, 32), (1, 16)))
    lower_upd = normal_values(keys[3], (LEAVES, SEP, GCOLS), SEP ** -0.5, 0.0625, ((0, 32), (1, 16)))
    upper_inv = normal_values(keys[4], (LEAVES, SEP, COLS), SEP ** -0.5, 0.0625, ((0, 32), (1, 16)))
    upper_upd = normal_values(keys[5], (LEAVES, SEP, GCOLS), SEP ** -0.5, 0.0625, ((0, 32), (1, 16)))
    return dict(forcing=forcing, live=live, lower_inv=lower_inv, lower_upd=lower_upd, upper_inv=upper_inv, upper_upd=upper_upd)


def level_shape(level):
    group = LEAVES >> (LEV - 1 - level)
    width = SEP // group
    offset = 2 * (SEP // (LEAVES >> (LEV - 1))) - 2 * width
    return group, width, offset


def node_matrix(panel, group, width, offset, node):
    block = panel[node * group:(node + 1) * group, :, offset:offset + width]
    return jnp.transpose(block, (1, 0, 2)).reshape(SEP, group * width)


def node_mask(live, level, node):
    return (jnp.arange(SEP) < live[level, node] * BLK).astype(jnp.float32)[:, None]


def reference(forcing, live, lower_inv, lower_upd, upper_inv, upper_upd):
    first_group = LEAVES >> (LEV - 1)
    residuals = []
    for node in range(LEAVES // first_group):
        piece = forcing[node * first_group:(node + 1) * first_group].astype(jnp.float32)
        residuals.append(jnp.sum(piece, axis=0))
    solved = []
    for level in range(LEV):
        group, width, offset = level_shape(level)
        count = LEAVES // group
        level_y = []
        updates = []
        for node in range(count):
            mask = node_mask(live, level, node)
            masked = (mask * residuals[node]).astype(jnp.bfloat16)
            inverse = node_matrix(lower_inv, group, width, offset, node)
            level_y.append((mask * jnp.dot(inverse, masked, preferred_element_type=jnp.float32)).astype(jnp.bfloat16))
            if level < LEV - 1:
                update = node_matrix(lower_upd, group, width, offset, node)
                updates.append(jnp.dot(update, masked, preferred_element_type=jnp.float32))
        solved.append(level_y)
        if level < LEV - 1:
            residuals = []
            for parent in range(count // 2):
                residuals.append(-updates[2 * parent] - updates[2 * parent + 1])
    results = [None] * LEV
    above = None
    for level in reversed(range(LEV)):
        group, width, offset = level_shape(level)
        count = LEAVES // group
        level_x = []
        for node in range(count):
            mask = node_mask(live, level, node)
            inverse = node_matrix(upper_inv, group, width, offset, node)
            term = jnp.dot(inverse, solved[level][node], preferred_element_type=jnp.float32)
            if above is not None:
                coupling = node_matrix(upper_upd, group, width, offset, node)
                term = term - jnp.dot(coupling, above[node // 2], preferred_element_type=jnp.float32)
            level_x.append((mask * term).astype(jnp.bfloat16))
        above = level_x
        results[level] = jnp.repeat(jnp.stack(level_x), group, axis=0)
    return jnp.stack(results)
```

```python
import jax
import jax.numpy as jnp
from jax import lax
from jax.sharding import PartitionSpec as P

BLK = 128
WIN = 24
PIECE = 40
LO = PIECE - WIN


def body(forcing, live, lower_inv, lower_upd, upper_inv, upper_upd):
    n_leaf = lax.axis_size("leaf")
    n_front = lax.axis_size("front")
    n_z = n_leaf // 2
    half = n_z // 2
    sep_dev, n_rhs = forcing.shape[1:]
    w0, w1 = sep_dev, sep_dev // 2
    leaf_id = lax.axis_index("leaf")
    front_id = lax.axis_index("front")
    z, core = leaf_id // 2, leaf_id % 2
    node, z8 = z // half, z % half
    bf, f32 = jnp.bfloat16, jnp.float32

    plane = [[(2 * k + c) * n_front + f for c in range(2) for f in range(n_front)] for k in range(n_z)]
    z_all = [[2 * k + c for k in range(n_z)] for c in range(2)]
    z_half = [[2 * (h * half + k) + c for k in range(half)] for h in range(2) for c in range(2)]
    leaf_half = [list(range(h * n_z, (h + 1) * n_z)) for h in range(2)]

    def a2a_plane(v):
        return lax.all_to_all(v, ("leaf", "front"), 0, 0, axis_index_groups=plane)

    def a2a_leaf(v, groups):
        return lax.all_to_all(v, "leaf", 0, 0, axis_index_groups=groups)

    def spread(v, n):
        return jnp.broadcast_to(v[None], (n,) + v.shape)

    def cut(v):
        v = v.reshape(n_front, PIECE, v.shape[-1])
        return jnp.concatenate([v[:, :WIN], v[:, LO:]], 0)

    def join(v):
        low, high = v[:n_front], v[n_front:, WIN - LO :]
        return jnp.concatenate([low, high], 1).reshape(n_front * PIECE, v.shape[-1])

    def total(v):
        return jnp.sum(v.astype(f32), 0)

    def piece_mask(first_block, n_blocks, count):
        rows = (
            (first_block + jnp.arange(n_blocks)[:, None]) * sep_dev
            + front_id * PIECE
            + core * LO
            + jnp.arange(WIN)[None, :]
        )
        return (rows < count * BLK).astype(f32)[:, :, None]

    def times(mat, vec):
        width = mat.shape[-1]
        m = mat.reshape(2, n_front * WIN, width)
        v = vec.reshape(2, width, n_rhs)
        return (
            jnp.dot(m[0], v[0], preferred_element_type=f32)
            + jnp.dot(m[1], v[1], preferred_element_type=f32)
        ).reshape(n_front, WIN, n_rhs)

    mask0 = piece_mask(2 * z8, 2, live[0][node])
    mask1 = piece_mask(z, 1, live[1][0])
    rows = front_id * sep_dev + jnp.arange(sep_dev)
    rows_mask = (rows < live[0][node] * BLK).astype(f32)[:, None]

    got = a2a_plane(cut(forcing[0]))
    low0 = a2a_plane(cut(jnp.concatenate([lower_upd[0], lower_inv[0]], 1)))
    up1 = a2a_plane(cut(upper_inv[0, :, w0:]))
    g0, linv0, linv1 = low0[:, :, :w0], low0[:, :, w0 : 2 * w0], low0[:, :, 2 * w0 :]

    pair = got[:n_front].astype(f32) + got[n_front:].astype(f32)
    pair = pair.astype(bf).reshape(half, 2 * WIN, n_rhs)
    r0 = total(a2a_leaf(pair, z_half)).reshape(2, WIN, n_rhs)
    rm0 = (mask0 * r0).astype(bf)

    def gather_two(v):
        got = a2a_plane(spread(v, 2 * n_front))
        return jnp.concatenate([join(got[:, 0]), join(got[:, 1])], 0)

    rm0 = gather_two(rm0)
    c_part = times(g0, rm0).astype(bf)
    y_part = times(linv0, rm0).astype(bf).reshape(half, 2 * WIN, n_rhs)
    zero = jnp.zeros_like(y_part)
    first = node == 0
    y_part = jnp.concatenate([jnp.where(first, y_part, zero), jnp.where(first, zero, y_part)], 0)
    got = total(a2a_leaf(jnp.concatenate([c_part, y_part], 1), z_all))
    r1 = (mask1[0] * -got[:WIN]).astype(bf)
    y0 = (mask0 * got[WIN:].reshape(2, WIN, n_rhs)).astype(bf)
    got = a2a_plane(spread(jnp.concatenate([r1[None], y0], 0), 2 * n_front))
    r1 = join(got[:, 0])
    y0 = jnp.concatenate([join(got[:, 1]), join(got[:, 2])], 0)

    y1 = total(a2a_leaf(times(linv1, r1).astype(bf), z_all))
    y1 = (mask1[0] * y1).astype(bf)
    y1 = join(a2a_plane(spread(y1, 2 * n_front)))

    x_part = times(up1, y1).astype(bf).reshape(half, 2 * WIN, n_rhs)
    x1 = total(a2a_leaf(jnp.concatenate([x_part, x_part], 0), z_all)).reshape(2, WIN, n_rhs)
    x1 = (piece_mask(2 * z8, 2, live[1][0]) * x1).astype(bf)
    x1_all = a2a_leaf(spread(x1, half), z_half).reshape(n_front, WIN, n_rhs)
    x1_out = join(a2a_plane(jnp.concatenate([x1_all, x1_all], 0)))
    x1 = gather_two(x1)

    y0 = lax.dynamic_slice_in_dim(y0, core * w0, w0, 0)
    x1 = lax.dynamic_slice_in_dim(x1, core * w0, w0, 0)
    term = jnp.dot(upper_inv[0, :, :w0], y0, preferred_element_type=f32) - jnp.dot(
        upper_upd[0], x1, preferred_element_type=f32
    )
    term = total(a2a_leaf(term.astype(bf).reshape(n_z, sep_dev // n_z, n_rhs), leaf_half))
    x0 = a2a_leaf(spread(term.astype(bf), n_z), leaf_half).reshape(sep_dev, n_rhs)
    x0 = (rows_mask * x0).astype(bf)
    return jnp.stack([x0, x1_out])[:, None]


def solution(mesh):
    return jax.shard_map(
        body,
        mesh=mesh,
        in_specs=(
            P("leaf", "front", None),
            P(),
            P("leaf", "front", None),
            P("leaf", "front", None),
            P("leaf", "front", None),
            P("leaf", "front", None),
        ),
        out_specs=P(None, "leaf", "front", None),
        check_vma=False,
    )
```

```python
import jax
import jax.numpy as jnp
from jax import lax
from jax.sharding import PartitionSpec as P

BLK = 128
WIN = 24
PIECE = 40
LO = PIECE - WIN


def body(forcing, live, lower_inv, lower_upd, upper_inv, upper_upd):
    n_leaf = lax.axis_size("leaf")
    n_front = lax.axis_size("front")
    n_z = n_leaf // 2
    half = n_z // 2
    sep_dev, n_rhs = forcing.shape[1:]
    w0, w1 = sep_dev, sep_dev // 2
    leaf_id = lax.axis_index("leaf")
    front_id = lax.axis_index("front")
    z, core = leaf_id // 2, leaf_id % 2
    node, z8 = z // half, z % half
    bf, f32 = jnp.bfloat16, jnp.float32

    plane = [[(2 * k + c) * n_front + f for c in range(2) for f in range(n_front)] for k in range(n_z)]
    z_all = [[2 * k + c for k in range(n_z)] for c in range(2)]
    z_half = [[2 * (h * half + k) + c for k in range(half)] for h in range(2) for c in range(2)]

    def a2a_plane(v):
        return lax.all_to_all(v, ("leaf", "front"), 0, 0, axis_index_groups=plane)

    def a2a_leaf(v, groups):
        return lax.all_to_all(v, "leaf", 0, 0, axis_index_groups=groups)

    def spread(v, n):
        return jnp.broadcast_to(v[None], (n,) + v.shape)

    def cut(v):
        v = v.reshape(n_front, PIECE, v.shape[-1])
        return jnp.concatenate([v[:, :WIN], v[:, LO:]], 0)

    def join(v):
        low, high = v[:n_front], v[n_front:, WIN - LO :]
        return jnp.concatenate([low, high], 1).reshape(n_front * PIECE, v.shape[-1])

    def total(v):
        return jnp.sum(v.astype(f32), 0)

    def piece_mask(first_block, n_blocks, count):
        rows = (
            (first_block + jnp.arange(n_blocks)[:, None]) * sep_dev
            + front_id * PIECE
            + core * LO
            + jnp.arange(WIN)[None, :]
        )
        return (rows < count * BLK).astype(f32)[:, :, None]

    def times(mat, vec):
        width = mat.shape[-1]
        m = mat.reshape(2, n_front * WIN, width)
        v = vec.reshape(2, width, n_rhs)
        return (
            jnp.dot(m[0], v[0], preferred_element_type=f32)
            + jnp.dot(m[1], v[1], preferred_element_type=f32)
        ).reshape(n_front, WIN, n_rhs)

    def fold(v):
        return v[:n_front].astype(f32) + v[n_front:].astype(f32)

    def by_core(v):
        return jnp.broadcast_to(v[:, None], (2, n_front) + v.shape[1:]).reshape((2 * n_front,) + v.shape[1:])

    swap = [(k, k ^ 1) for k in range(n_leaf)]
    mask0 = piece_mask(2 * z8, 2, live[0][node])
    mask1 = piece_mask(z, 1, live[1][0])

    got = a2a_plane(cut(forcing[0]))
    pair = fold(got).astype(bf).reshape(half, 2 * WIN, n_rhs)
    r0 = total(a2a_leaf(pair, z_half)).reshape(2, WIN, n_rhs)
    rm0 = join(a2a_plane(by_core((mask0 * r0).astype(bf))))

    c_part = jnp.dot(lower_upd[0], rm0, preferred_element_type=f32).astype(bf)
    y_part = jnp.dot(lower_inv[0, :, :w0], rm0, preferred_element_type=f32).astype(bf)
    root = cut(jnp.concatenate([lower_inv[0, :, w0:], upper_inv[0, :, w0:]], 1))
    got = a2a_plane(jnp.concatenate([cut(jnp.concatenate([c_part, y_part], 1)), root], 2))
    parts = fold(got[:, :, : 2 * n_rhs]).astype(bf)
    linv1 = got[:, :, 2 * n_rhs : 2 * n_rhs + w1]
    uinv1 = got[:, :, 2 * n_rhs + w1 :]

    c_part = parts[:, :, :n_rhs]
    y_part = parts[:, :, n_rhs:].reshape(half, 2 * WIN, n_rhs)
    zero = jnp.zeros_like(y_part)
    first = node == 0
    y_part = jnp.concatenate([jnp.where(first, y_part, zero), jnp.where(first, zero, y_part)], 0)
    got = total(a2a_leaf(jnp.concatenate([c_part, y_part], 1), z_all))
    r1 = (mask1[0] * -got[:WIN]).astype(bf)
    y0 = (mask0 * got[WIN:].reshape(2, WIN, n_rhs)).astype(bf)
    got = a2a_plane(by_core(jnp.concatenate([jnp.stack([r1, r1]), y0], 1)))
    r1 = join(got[:, :WIN])
    y0 = join(got[:, WIN:])

    y1 = total(a2a_leaf(times(linv1, r1).astype(bf), z_all))
    y1 = (mask1[0] * y1).astype(bf)
    y1 = join(a2a_plane(spread(y1, 2 * n_front)))

    x_part = times(uinv1, y1).astype(bf).reshape(half, 2 * WIN, n_rhs)
    x1 = total(a2a_leaf(jnp.concatenate([x_part, x_part], 0), z_all)).reshape(2, WIN, n_rhs)
    x1 = (piece_mask(2 * z8, 2, live[1][0]) * x1).astype(bf)
    x1c = join(a2a_plane(by_core(x1)))

    term = jnp.dot(upper_inv[0, :, :w0], y0, preferred_element_type=f32) - jnp.dot(
        upper_upd[0], x1c, preferred_element_type=f32
    )
    term = term.reshape(2, half, PIECE, n_rhs)
    away = lax.dynamic_index_in_dim(term, 1 - core, 0, False).astype(bf)
    keep = lax.dynamic_index_in_dim(term, core, 0, False)
    term = (keep + lax.ppermute(away, "leaf", swap).astype(f32)).astype(bf)
    got = a2a_leaf(jnp.concatenate([term, spread(x1.reshape(2 * WIN, n_rhs), half)], 1), z_half)
    x1_out = got[:, PIECE:].reshape(n_front, WIN, n_rhs)
    x1_out = join(a2a_plane(jnp.concatenate([x1_out, x1_out], 0)))

    rows = front_id * sep_dev + (core * half + z8) * PIECE + jnp.arange(PIECE)
    x0 = total(got[:, :PIECE]) * (rows < live[0][node] * BLK).astype(f32)[:, None]
    x0 = a2a_leaf(spread(x0.astype(bf), half), z_half).reshape(half * PIECE, n_rhs)
    other = lax.ppermute(x0, "leaf", swap)
    x0 = jnp.where(core == 0, jnp.concatenate([x0, other], 0), jnp.concatenate([other, x0], 0))
    return jnp.stack([x0, x1_out])[:, None]


def solution(mesh):
    return jax.shard_map(
        body,
        mesh=mesh,
        in_specs=(
            P("leaf", "front", None),
            P(),
            P("leaf", "front", None),
            P("leaf", "front", None),
            P("leaf", "front", None),
            P("leaf", "front", None),
        ),
        out_specs=P(None, "leaf", "front", None),
        check_vma=False,
    )
```

```python
import jax
import jax.numpy as jnp
from jax import lax
from jax.sharding import PartitionSpec as P

BLK = 128
WIN = 24
PIECE = 40
LO = PIECE - WIN


def body(forcing, live, lower_inv, lower_upd, upper_inv, upper_upd):
    n_leaf = lax.axis_size("leaf")
    n_front = lax.axis_size("front")
    n_z = n_leaf // 2
    half = n_z // 2
    sep_dev, n_rhs = forcing.shape[1:]
    w0, w1 = sep_dev, sep_dev // 2
    leaf_id = lax.axis_index("leaf")
    front_id = lax.axis_index("front")
    z, core = leaf_id // 2, leaf_id % 2
    node, z8 = z // half, z % half
    bf, f32 = jnp.bfloat16, jnp.float32

    plane = [[(2 * k + c) * n_front + f for c in range(2) for f in range(n_front)] for k in range(n_z)]
    z_all = [[2 * k + c for k in range(n_z)] for c in range(2)]
    z_half = [[2 * (h * half + k) + c for k in range(half)] for h in range(2) for c in range(2)]

    def a2a_plane(v):
        return lax.all_to_all(v, ("leaf", "front"), 0, 0, axis_index_groups=plane)

    def a2a_leaf(v, groups):
        return lax.all_to_all(v, "leaf", 0, 0, axis_index_groups=groups)

    def spread(v, n):
        return jnp.broadcast_to(v[None], (n,) + v.shape)

    def cut(v):
        v = v.reshape(n_front, PIECE, v.shape[-1])
        return jnp.concatenate([v[:, :WIN], v[:, LO:]], 0)

    def join(v):
        low, high = v[:n_front], v[n_front:, WIN - LO :]
        return jnp.concatenate([low, high], 1).reshape(n_front * PIECE, v.shape[-1])

    def total(v):
        return jnp.sum(v.astype(f32), 0)

    def piece_mask(first_block, n_blocks, count):
        rows = (
            (first_block + jnp.arange(n_blocks)[:, None]) * sep_dev
            + front_id * PIECE
            + core * LO
            + jnp.arange(WIN)[None, :]
        )
        return (rows < count * BLK).astype(f32)[:, :, None]

    def times(mat, vec):
        width = mat.shape[-1]
        m = mat.reshape(2, n_front * WIN, width)
        v = vec.reshape(2, width, n_rhs)
        return (
            jnp.dot(m[0], v[0], preferred_element_type=f32)
            + jnp.dot(m[1], v[1], preferred_element_type=f32)
        ).reshape(n_front, WIN, n_rhs)

    def fold(v):
        return v[:n_front].astype(f32) + v[n_front:].astype(f32)

    def by_core(v):
        return jnp.broadcast_to(v[:, None], (2, n_front) + v.shape[1:]).reshape((2 * n_front,) + v.shape[1:])

    swap = [(k, k ^ 1) for k in range(n_leaf)]
    mask0 = piece_mask(2 * z8, 2, live[0][node])
    mask1 = piece_mask(z, 1, live[1][0])

    got = a2a_plane(cut(forcing[0]))
    pair = fold(got).astype(bf).reshape(half, 2 * WIN, n_rhs)
    r0 = total(a2a_leaf(pair, z_half)).reshape(2, WIN, n_rhs)
    rm0 = join(a2a_plane(by_core((mask0 * r0).astype(bf))))

    c_part = jnp.dot(lower_upd[0], rm0, preferred_element_type=f32).astype(bf)
    y_part = jnp.dot(lower_inv[0, :, :w0], rm0, preferred_element_type=f32).astype(bf)
    root = cut(jnp.concatenate([lower_inv[0, :, w0:], upper_inv[0, :, w0:]], 1))
    got = a2a_plane(jnp.concatenate([cut(jnp.concatenate([c_part, y_part], 1)), root], 2))
    parts = fold(got[:, :, : 2 * n_rhs]).astype(bf)
    linv1 = got[:, :, 2 * n_rhs : 2 * n_rhs + w1]
    uinv1 = got[:, :, 2 * n_rhs + w1 :]

    c_part = parts[:, :, :n_rhs]
    y_part = parts[:, :, n_rhs:].reshape(half, 2 * WIN, n_rhs)
    zero = jnp.zeros_like(y_part)
    first = node == 0
    y_part = jnp.concatenate([jnp.where(first, y_part, zero), jnp.where(first, zero, y_part)], 0)
    got = total(a2a_leaf(jnp.concatenate([c_part, y_part], 1), z_all))
    r1 = (mask1[0] * -got[:WIN]).astype(bf)
    y0 = (mask0 * got[WIN:].reshape(2, WIN, n_rhs)).astype(bf)
    got = a2a_plane(by_core(jnp.concatenate([jnp.stack([r1, r1]), y0], 1)))
    r1 = join(got[:, :WIN])
    y0 = join(got[:, WIN:])

    y1 = total(a2a_leaf(times(linv1, r1).astype(bf), z_all))
    y1 = (mask1[0] * y1).astype(bf)
    y1 = join(a2a_plane(spread(y1, 2 * n_front)))

    x_part = times(uinv1, y1).astype(bf).reshape(half, 2 * WIN, n_rhs)
    x1 = total(a2a_leaf(jnp.concatenate([x_part, x_part], 0), z_all)).reshape(2, WIN, n_rhs)
    x1 = (piece_mask(2 * z8, 2, live[1][0]) * x1).astype(bf)
    own = jnp.broadcast_to(x1[None, None], (2, n_front // 2) + x1.shape).reshape(2 * n_front, WIN, n_rhs)
    got = a2a_plane(jnp.concatenate([by_core(x1), own], 1))
    x1c = join(got[:, :WIN])
    own = join(got[:, WIN:])

    term = jnp.dot(upper_inv[0, :, :w0], y0, preferred_element_type=f32) - jnp.dot(
        upper_upd[0], x1c, preferred_element_type=f32
    )
    term = term.reshape(2, half, PIECE, n_rhs)
    away = lax.dynamic_index_in_dim(term, 1 - core, 0, False).astype(bf)
    keep = lax.dynamic_index_in_dim(term, core, 0, False)
    term = (keep + lax.ppermute(away, "leaf", swap).astype(f32)).astype(bf)
    own = lax.dynamic_index_in_dim(own.reshape(2, half, PIECE, n_rhs), core, 0, False)
    got = a2a_leaf(jnp.concatenate([term, own], 1), z_half)

    rows = front_id * sep_dev + (core * half + z8) * PIECE + jnp.arange(PIECE)
    x0 = total(got[:, :PIECE]) * (rows < live[0][node] * BLK).astype(f32)[:, None]
    x1 = lax.dynamic_index_in_dim(got[:, PIECE:], front_id // 2, 0, False)
    both = a2a_leaf(spread(jnp.stack([x0.astype(bf), x1]), half), z_half)
    both = jnp.swapaxes(both, 0, 1).reshape(2, half * PIECE, n_rhs)
    other = lax.ppermute(both, "leaf", swap)
    both = jnp.where(core == 0, jnp.concatenate([both, other], 1), jnp.concatenate([other, both], 1))
    return both[:, None]


def solution(mesh):
    return jax.shard_map(
        body,
        mesh=mesh,
        in_specs=(
            P("leaf", "front", None),
            P(),
            P("leaf", "front", None),
            P("leaf", "front", None),
            P("leaf", "front", None),
            P("leaf", "front", None),
        ),
        out_specs=P(None, "leaf", "front", None),
        check_vma=False,
    )
```

```python
import jax
import jax.numpy as jnp
from jax import lax
from jax.sharding import PartitionSpec as P

BLK = 128
WIN = 24
PIECE = 40
LO = PIECE - WIN


def body(forcing, live, lower_inv, lower_upd, upper_inv, upper_upd):
    n_leaf = lax.axis_size("leaf")
    n_front = lax.axis_size("front")
    n_z = n_leaf // 2
    half = n_z // 2
    sep_dev, n_rhs = forcing.shape[1:]
    w0, w1 = sep_dev, sep_dev // 2
    leaf_id = lax.axis_index("leaf")
    front_id = lax.axis_index("front")
    z, core = leaf_id // 2, leaf_id % 2
    node, z8 = z // half, z % half
    bf, f32 = jnp.bfloat16, jnp.float32

    plane = [[(2 * k + c) * n_front + f for c in range(2) for f in range(n_front)] for k in range(n_z)]
    z_all = [[2 * k + c for k in range(n_z)] for c in range(2)]
    z_half = [[2 * (h * half + k) + c for k in range(half)] for h in range(2) for c in range(2)]

    def a2a_plane(v):
        return lax.all_to_all(v, ("leaf", "front"), 0, 0, axis_index_groups=plane)

    def a2a_leaf(v, groups):
        return lax.all_to_all(v, "leaf", 0, 0, axis_index_groups=groups)

    def spread(v, n):
        return jnp.broadcast_to(v[None], (n,) + v.shape)

    def cut(v):
        v = v.reshape(n_front, PIECE, v.shape[-1])
        return jnp.concatenate([v[:, :WIN], v[:, LO:]], 0)

    def join(v):
        low, high = v[:n_front], v[n_front:, WIN - LO :]
        return jnp.concatenate([low, high], 1).reshape(n_front * PIECE, v.shape[-1])

    def total(v):
        return jnp.sum(v.astype(f32), 0)

    def piece_mask(first_block, n_blocks, count):
        rows = (
            (first_block + jnp.arange(n_blocks)[:, None]) * sep_dev
            + front_id * PIECE
            + core * LO
            + jnp.arange(WIN)[None, :]
        )
        return (rows < count * BLK).astype(f32)[:, :, None]

    def times(mat, vec):
        height = n_front * WIN
        m = mat.reshape(2 * height, mat.shape[-1])
        v = vec.reshape(2, vec.shape[0] // 2, n_rhs)
        return (
            jnp.dot(m[:height, n_rhs:], v[0], preferred_element_type=f32)
            + jnp.dot(m[height:, n_rhs:], v[1], preferred_element_type=f32)
        ).reshape(n_front, WIN, n_rhs)

    def fold(v):
        return v[:n_front].astype(f32) + v[n_front:].astype(f32)

    def by_core(v):
        return jnp.broadcast_to(v[:, None], (2, n_front) + v.shape[1:]).reshape((2 * n_front,) + v.shape[1:])

    swap = [(k, k ^ 1) for k in range(n_leaf)]
    rows = front_id * sep_dev + (core * half + z8) * PIECE + jnp.arange(PIECE)
    mask0 = piece_mask(2 * z8, 2, live[0][node])
    mask1 = piece_mask(z, 1, live[1][0])[0]
    mask2 = piece_mask(2 * z8, 2, live[1][0])
    mask3 = (rows < live[0][node] * BLK).astype(f32)[:, None]

    got = a2a_plane(cut(forcing[0]))
    linv1, uinv1 = cut(lower_inv[0, :, w0:]), cut(upper_inv[0, :, w0:])
    got, linv1, uinv1, mask0, mask1, mask2, mask3 = lax.optimization_barrier(
        (got, linv1, uinv1, mask0, mask1, mask2, mask3)
    )
    pair = fold(got).astype(bf).reshape(half, 2 * WIN, n_rhs)
    r0 = total(a2a_leaf(pair, z_half)).reshape(2, WIN, n_rhs)
    got = a2a_plane(jnp.concatenate([by_core((mask0 * r0).astype(bf)), linv1], 2))
    rm0 = join(got[:, :, :n_rhs])
    linv1 = got

    c_part = jnp.dot(lower_upd[0], rm0, preferred_element_type=f32).astype(bf)
    y_part = jnp.dot(lower_inv[0, :, :w0], rm0, preferred_element_type=f32).astype(bf)
    parts = fold(a2a_plane(cut(jnp.concatenate([c_part, y_part], 1)))).astype(bf)

    c_part = parts[:, :, :n_rhs]
    y_part = parts[:, :, n_rhs:].reshape(half, 2 * WIN, n_rhs)
    zero = jnp.zeros_like(y_part)
    first = node == 0
    y_part = jnp.concatenate([jnp.where(first, y_part, zero), jnp.where(first, zero, y_part)], 0)
    got = total(a2a_leaf(jnp.concatenate([c_part, y_part], 1), z_all))
    r1 = (mask1 * -got[:WIN]).astype(bf)
    y0 = (mask0 * got[WIN:].reshape(2, WIN, n_rhs)).astype(bf)
    got = a2a_plane(by_core(jnp.concatenate([jnp.stack([r1, r1]), y0], 1)))
    r1 = join(got[:, :WIN])
    y0 = join(got[:, WIN:])

    y1 = total(a2a_leaf(times(linv1, r1).astype(bf), z_all))
    y1 = (mask1 * y1).astype(bf)
    got = a2a_plane(jnp.concatenate([spread(y1, 2 * n_front), uinv1], 2))
    y1 = join(got[:, :, :n_rhs])

    x_part = times(got, y1).astype(bf).reshape(half, 2 * WIN, n_rhs)
    x1 = total(a2a_leaf(jnp.concatenate([x_part, x_part], 0), z_all)).reshape(2, WIN, n_rhs)
    x1 = (mask2 * x1).astype(bf)
    own = jnp.broadcast_to(x1[None, None], (2, n_front // 2) + x1.shape).reshape(2 * n_front, WIN, n_rhs)
    got = a2a_plane(jnp.concatenate([by_core(x1), own], 1))
    got, y0 = lax.optimization_barrier((got, y0))
    x1c = join(got[:, :WIN])
    own = join(got[:, WIN:])

    term = jnp.dot(upper_inv[0, :, :w0], y0, preferred_element_type=f32) - jnp.dot(
        upper_upd[0], x1c, preferred_element_type=f32
    )
    term = term.reshape(2, half, PIECE, n_rhs)
    away = lax.dynamic_index_in_dim(term, 1 - core, 0, False).astype(bf)
    keep = lax.dynamic_index_in_dim(term, core, 0, False)
    term = (keep + lax.ppermute(away, "leaf", swap).astype(f32)).astype(bf)
    own = lax.dynamic_index_in_dim(own.reshape(2, half, PIECE, n_rhs), core, 0, False)
    got = a2a_leaf(jnp.concatenate([term, own], 1), z_half)

    x0 = total(got[:, :PIECE]) * mask3
    x1 = lax.dynamic_index_in_dim(got[:, PIECE:], front_id // 2, 0, False)
    both = a2a_leaf(spread(jnp.stack([x0.astype(bf), x1]), half), z_half)
    both = jnp.swapaxes(both, 0, 1).reshape(2, half * PIECE, n_rhs)
    other = lax.ppermute(both, "leaf", swap)
    both = jnp.where(core == 0, jnp.concatenate([both, other], 1), jnp.concatenate([other, both], 1))
    return both[:, None]


def solution(mesh):
    return jax.shard_map(
        body,
        mesh=mesh,
        in_specs=(
            P("leaf", "front", None),
            P(),
            P("leaf", "front", None),
            P("leaf", "front", None),
            P("leaf", "front", None),
            P("leaf", "front", None),
        ),
        out_specs=P(None, "leaf", "front", None),
        check_vma=False,
    )
```

```python
import jax
import jax.numpy as jnp
from jax import lax
from jax.sharding import PartitionSpec as P

BLK = 128
WIN = 24
PIECE = 40
LO = PIECE - WIN


def body(forcing, live, lower_inv, lower_upd, upper_inv, upper_upd):
    n_leaf = lax.axis_size("leaf")
    n_front = lax.axis_size("front")
    n_z = n_leaf // 2
    half = n_z // 2
    sep_dev, n_rhs = forcing.shape[1:]
    w0, w1 = sep_dev, sep_dev // 2
    leaf_id = lax.axis_index("leaf")
    front_id = lax.axis_index("front")
    z, core = leaf_id // 2, leaf_id % 2
    node, z8 = z // half, z % half
    bf, f32 = jnp.bfloat16, jnp.float32

    plane = [[(2 * k + c) * n_front + f for c in range(2) for f in range(n_front)] for k in range(n_z)]
    z_all = [[2 * k + c for k in range(n_z)] for c in range(2)]
    z_half = [[2 * (h * half + k) + c for k in range(half)] for h in range(2) for c in range(2)]

    def a2a_plane(v):
        return lax.all_to_all(v, ("leaf", "front"), 0, 0, axis_index_groups=plane)

    def a2a_leaf(v, groups):
        return lax.all_to_all(v, "leaf", 0, 0, axis_index_groups=groups)

    def spread(v, n):
        return jnp.broadcast_to(v[None], (n,) + v.shape)

    def cut(v):
        v = v.reshape(n_front, PIECE, v.shape[-1])
        return jnp.concatenate([v[:, :WIN], v[:, LO:]], 0)

    def join(v):
        low, high = v[:n_front], v[n_front:, WIN - LO :]
        return jnp.concatenate([low, high], 1).reshape(n_front * PIECE, v.shape[-1])

    def total(v):
        return jnp.sum(v.astype(f32), 0)

    def piece_mask(first_block, n_blocks, count):
        rows = (
            (first_block + jnp.arange(n_blocks)[:, None]) * sep_dev
            + front_id * PIECE
            + core * LO
            + jnp.arange(WIN)[None, :]
        )
        return (rows < count * BLK).astype(f32)[:, :, None]

    def times(mat, vec):
        height = n_front * WIN
        m = mat.reshape(2 * height, mat.shape[-1])
        v = vec.reshape(2, vec.shape[0] // 2, n_rhs)
        return (
            jnp.dot(m[:height, n_rhs:], v[0], preferred_element_type=f32)
            + jnp.dot(m[height:, n_rhs:], v[1], preferred_element_type=f32)
        ).reshape(n_front, WIN, n_rhs)

    def fold(v):
        return v[:n_front].astype(f32) + v[n_front:].astype(f32)

    def by_core(v):
        return jnp.broadcast_to(v[:, None], (2, n_front) + v.shape[1:]).reshape((2 * n_front,) + v.shape[1:])

    swap = [(k, k ^ 1) for k in range(n_leaf)]
    rows = front_id * sep_dev + (core * half + z8) * PIECE + jnp.arange(PIECE)
    mask0 = piece_mask(2 * z8, 2, live[0][node])
    mask1 = piece_mask(z, 1, live[1][0])[0]
    mask2 = piece_mask(2 * z8, 2, live[1][0])
    mask4 = jnp.stack([piece_mask(z, 1, live[0][0]), piece_mask(z, 1, live[0][1])])[:, 0]
    mask3 = (rows < live[0][node] * BLK).astype(f32)[:, None]

    got = a2a_plane(cut(forcing[0]))
    linv1, uinv1 = cut(lower_inv[0, :, w0:]), cut(upper_inv[0, :, w0:])
    got, linv1, uinv1, mask0, mask1, mask2, mask3, mask4 = lax.optimization_barrier(
        (got, linv1, uinv1, mask0, mask1, mask2, mask3, mask4)
    )
    pair = fold(got).astype(bf).reshape(half, 2 * WIN, n_rhs)
    r0 = total(a2a_leaf(pair, z_half)).reshape(2, WIN, n_rhs)
    got = a2a_plane(jnp.concatenate([by_core((mask0 * r0).astype(bf)), linv1], 2))
    rm0 = join(got[:, :, :n_rhs])
    linv1 = got

    c_part = jnp.dot(lower_upd[0], rm0, preferred_element_type=f32).astype(bf)
    y_part = jnp.dot(lower_inv[0, :, :w0], rm0, preferred_element_type=f32).astype(bf)
    parts = fold(a2a_plane(cut(jnp.concatenate([c_part, y_part], 1)))).astype(bf)

    got = a2a_leaf(jnp.concatenate([parts[:, :, :n_rhs], parts[:, :, n_rhs:]], 1), z_all)
    r1 = (mask1 * -total(got[:, :WIN])).astype(bf)
    y0 = got[:, WIN:].reshape(2, half, WIN, n_rhs)
    y0 = (mask4 * jnp.sum(y0.astype(f32), 1)).astype(bf)
    r1 = join(a2a_plane(spread(r1, 2 * n_front)))

    y0 = jnp.broadcast_to(y0[:, None], (2, half, WIN, n_rhs)).reshape(n_z, WIN, n_rhs)
    got = a2a_leaf(jnp.concatenate([times(linv1, r1).astype(bf), y0], 1), z_all)
    y1 = (mask1 * total(got[:, :WIN])).astype(bf)
    y0 = lax.dynamic_slice_in_dim(got[:, WIN:], 2 * z8, 2, 0)
    got = a2a_plane(jnp.concatenate([spread(y1, 2 * n_front), uinv1], 2))
    y1 = join(got[:, :, :n_rhs])

    x_part = times(got, y1).astype(bf).reshape(half, 2 * WIN, n_rhs)
    x1 = total(a2a_leaf(jnp.concatenate([x_part, x_part], 0), z_all)).reshape(2, WIN, n_rhs)
    x1 = (mask2 * x1).astype(bf)
    own = jnp.broadcast_to(x1[None, None], (2, n_front // 2) + x1.shape).reshape(2 * n_front, WIN, n_rhs)
    got = a2a_plane(jnp.concatenate([by_core(x1), own, by_core(y0)], 1))
    x1c = join(got[:, :WIN])
    own = join(got[:, WIN : 2 * WIN])
    y0 = join(got[:, 2 * WIN :])

    term = jnp.dot(upper_inv[0, :, :w0], y0, preferred_element_type=f32) - jnp.dot(
        upper_upd[0], x1c, preferred_element_type=f32
    )
    term = term.reshape(2, half, PIECE, n_rhs)
    away = lax.dynamic_index_in_dim(term, 1 - core, 0, False).astype(bf)
    keep = lax.dynamic_index_in_dim(term, core, 0, False)
    term = (keep + lax.ppermute(away, "leaf", swap).astype(f32)).astype(bf)
    own = lax.dynamic_index_in_dim(own.reshape(2, half, PIECE, n_rhs), core, 0, False)
    got = a2a_leaf(jnp.concatenate([term, own], 1), z_half)

    x0 = total(got[:, :PIECE]) * mask3
    x1 = lax.dynamic_index_in_dim(got[:, PIECE:], front_id // 2, 0, False)
    both = a2a_leaf(spread(jnp.stack([x0.astype(bf), x1]), half), z_half)
    both = jnp.swapaxes(both, 0, 1).reshape(2, half * PIECE, n_rhs)
    other = lax.ppermute(both, "leaf", swap)
    both = jnp.where(core == 0, jnp.concatenate([both, other], 1), jnp.concatenate([other, both], 1))
    return both[:, None]


def solution(mesh):
    return jax.shard_map(
        body,
        mesh=mesh,
        in_specs=(
            P("leaf", "front", None),
            P(),
            P("leaf", "front", None),
            P("leaf", "front", None),
            P("leaf", "front", None),
            P("leaf", "front", None),
        ),
        out_specs=P(None, "leaf", "front", None),
        check_vma=False,
    )
```

```python
import jax
import jax.numpy as jnp
from jax import lax
from jax.sharding import PartitionSpec as P

BLK = 128
WIN = 24
PIECE = 40
LO = PIECE - WIN


def body(forcing, live, lower_inv, lower_upd, upper_inv, upper_upd):
    n_leaf = lax.axis_size("leaf")
    n_front = lax.axis_size("front")
    n_z = n_leaf // 2
    half = n_z // 2
    sep_dev, n_rhs = forcing.shape[1:]
    w0, w1 = sep_dev, sep_dev // 2
    n_plane = 2 * n_front
    height = n_front * WIN
    tail = w1 % n_rhs
    head = w1 - tail
    bf, f32, i32, u32 = jnp.bfloat16, jnp.float32, jnp.int32, jnp.uint32
    leaf_id = lax.axis_index("leaf").astype(u32)
    front_id = lax.axis_index("front").astype(u32)
    z, core = leaf_id // 2, leaf_id % 2
    node, z8 = z // half, z % half

    plane = [[(2 * k + c) * n_front + f for c in range(2) for f in range(n_front)] for k in range(n_z)]
    z_all = [[2 * k + c for k in range(n_z)] for c in range(2)]
    z_half = [[2 * (h * half + k) + c for k in range(half)] for h in range(2) for c in range(2)]
    swap = [(k, k ^ 1) for k in range(n_leaf)]

    def a2a_plane(v):
        return lax.all_to_all(v, ("leaf", "front"), 0, 0, axis_index_groups=plane)

    def a2a_leaf(v, groups):
        return lax.all_to_all(v, "leaf", 0, 0, axis_index_groups=groups)

    def spread(v, n):
        return jnp.broadcast_to(v[None], (n,) + v.shape)

    def by_core(v):
        return jnp.broadcast_to(v[:, None], (2, n_front) + v.shape[1:]).reshape((n_plane,) + v.shape[1:])

    def cut(v):
        v = v.reshape(n_front, PIECE, v.shape[-1])
        return jnp.concatenate([v[:, :WIN], v[:, LO:]], 0)

    def join(v):
        low, high = v[:n_front], v[n_front:, WIN - LO :]
        return jnp.concatenate([low, high], 1).reshape(n_front * PIECE, v.shape[-1])

    def fold(v):
        return v[:n_front].astype(f32) + v[n_front:].astype(f32)

    def total(v):
        return jnp.sum(v.astype(f32), 0)

    def pick(v, k, n):
        return lax.dynamic_slice(v, (k,) + (u32(0),) * (v.ndim - 1), (n,) + v.shape[1:])

    def masked(v, keep):
        return jnp.where(keep[..., None], v, 0.0).astype(bf)

    def dot(a, b):
        return jnp.dot(a, b, preferred_element_type=f32)

    def panel(mat, h, first, last):
        return mat.reshape(2 * height, mat.shape[-1])[h * height : (h + 1) * height, first:last]

    live_a, live_b, live_root = (live[k].reshape(()) * BLK for k in ((0, slice(0, 1)), (0, slice(1, 2)), (1, slice(0, 1))))
    live_node = jnp.where(node == 0, live_a, live_b)
    here = (front_id * PIECE + core * LO).astype(i32)
    at_out = (front_id * sep_dev + (core * half + z8) * PIECE).astype(i32)
    kind = lax.iota(i32, 8)
    count = jnp.where(kind == 2, live_a, jnp.where(kind == 3, live_b, jnp.where((kind < 4) | (kind > 6), live_node, live_root)))
    block = jnp.where((kind > 1) & (kind < 5), z.astype(i32), 2 * z8.astype(i32) + ((kind == 1) | (kind == 6)).astype(i32))
    begin = jnp.where(kind == 7, at_out, here + block * sep_dev)
    keep = lax.broadcasted_iota(i32, (8, PIECE), 1) < (count - begin)[:, None]
    keep = (keep[0:2, :WIN], keep[2, :WIN], keep[3, :WIN], keep[4, :WIN], keep[5:7, :WIN], keep[7])
    scalars = (keep, core, 1 - core, 2 * z8, front_id // 2)

    got = a2a_plane(cut(forcing[0]))
    uinv1 = cut(upper_inv[0, :, w0:])
    extra = jnp.concatenate([cut(lower_inv[0, :, w0:]), uinv1[:, :, head:]], 2)
    got, extra, uinv1, scalars = lax.optimization_barrier((got, extra, uinv1[:, :, :head], scalars))
    keep, core, other_core, two_z8, half_front = scalars

    pair = fold(got).astype(bf).reshape(half, 2 * WIN, n_rhs)
    r0 = total(a2a_leaf(pair, z_half)).reshape(2, WIN, n_rhs)
    moved = a2a_plane(jnp.concatenate([by_core(masked(r0, keep[0])), extra], 2))
    rm0 = join(moved[:, :, :n_rhs])

    c_part = dot(lower_upd[0], rm0).astype(bf)
    y_part = dot(lower_inv[0, :, :w0], rm0).astype(bf)
    parts = fold(a2a_plane(cut(jnp.concatenate([c_part, y_part], 1)))).astype(bf)

    got = a2a_leaf(jnp.concatenate([parts[:, :, :n_rhs], parts[:, :, n_rhs:]], 1), z_all)
    r1 = masked(-total(got[:, :WIN]), keep[3])
    y0 = jnp.stack([masked(total(got[:half, WIN:]), keep[1]), masked(total(got[half:, WIN:]), keep[2])])
    y0 = jnp.broadcast_to(y0[:, None], (2, half, WIN, n_rhs)).reshape(n_z, WIN, n_rhs)
    r1, y0 = lax.optimization_barrier((spread(r1, n_plane), y0))
    r1 = join(a2a_plane(r1))

    blank = jnp.zeros((n_rhs - tail, n_rhs), bf)
    y1 = sum(
        dot(panel(moved, h, n_rhs, n_rhs + w1 + tail), jnp.concatenate([r1[h * w1 : (h + 1) * w1], blank], 0))
        for h in range(2)
    )
    got = a2a_leaf(jnp.concatenate([y1.astype(bf).reshape(n_front, WIN, n_rhs), y0], 1), z_all)
    y1 = masked(total(got[:, :WIN]), keep[3])
    y0 = pick(got[:, WIN:], two_z8, 2)
    got = a2a_plane(jnp.concatenate([spread(y1, n_plane), by_core(y0), uinv1], 2))
    y1 = join(got[:, :, :n_rhs])
    y0 = join(got[:, :, n_rhs : 2 * n_rhs])

    x1 = 0.0
    for h in range(2):
        v = y1[h * w1 : (h + 1) * w1]
        x1 = x1 + dot(panel(got, h, 2 * n_rhs, 2 * n_rhs + head), v[:head])
        x1 = x1 + dot(panel(moved, h, n_rhs + head, n_rhs + head + n_rhs), jnp.concatenate([blank, v[head:]], 0))
    x1 = x1.astype(bf).reshape(half, 2 * WIN, n_rhs)
    x1, term = lax.optimization_barrier((jnp.concatenate([x1, x1], 0), dot(upper_inv[0, :, :w0], y0)))
    x1 = masked(total(a2a_leaf(x1, z_all)).reshape(2, WIN, n_rhs), keep[4])
    own = jnp.broadcast_to(x1[None, None], (2, n_front // 2) + x1.shape).reshape(n_plane, WIN, n_rhs)
    got = a2a_plane(jnp.concatenate([by_core(x1), own], 1))
    x1 = join(got[:, :WIN])
    own = join(got[:, WIN:])

    term = (term - dot(upper_upd[0], x1)).reshape(2, half, PIECE, n_rhs)
    away = pick(term, other_core, 1)[0].astype(bf)
    own = pick(own.reshape(2, half, PIECE, n_rhs), core, 1)[0]
    away = lax.ppermute(away, "leaf", swap)
    term = (pick(term, core, 1)[0] + away.astype(f32)).astype(bf)
    got = a2a_leaf(jnp.concatenate([term, own], 1), z_half)

    x0 = masked(total(got[:, :PIECE]), keep[5])
    x1 = pick(got[:, PIECE:], half_front, 1)[0]
    both = a2a_leaf(spread(jnp.stack([x0, x1]), half), z_half)
    both = jnp.swapaxes(both, 0, 1).reshape(2, half * PIECE, n_rhs)
    other = lax.ppermute(both, "leaf", swap)
    both = jnp.where(core == 0, jnp.concatenate([both, other], 1), jnp.concatenate([other, both], 1))
    return both[:, None]


def solution(mesh):
    return jax.shard_map(
        body,
        mesh=mesh,
        in_specs=(
            P("leaf", "front", None),
            P(),
            P("leaf", "front", None),
            P("leaf", "front", None),
            P("leaf", "front", None),
            P("leaf", "front", None),
        ),
        out_specs=P(None, "leaf", "front", None),
        check_vma=False,
    )
```

```python
import jax
import jax.numpy as jnp
from jax import lax
from jax.sharding import PartitionSpec as P

BLK = 128
WIN = 24
PIECE = 40
LO = PIECE - WIN


def body(forcing, live, lower_inv, lower_upd, upper_inv, upper_upd):
    n_leaf = lax.axis_size("leaf")
    n_front = lax.axis_size("front")
    n_z = n_leaf // 2
    half = n_z // 2
    sep_dev, n_rhs = forcing.shape[1:]
    w0, w1 = sep_dev, sep_dev // 2
    n_plane = 2 * n_front
    height = n_front * WIN
    tail = w1 % n_rhs
    head = w1 - tail
    bf, f32, i32, u32 = jnp.bfloat16, jnp.float32, jnp.int32, jnp.uint32
    leaf_id = lax.axis_index("leaf").astype(u32)
    front_id = lax.axis_index("front").astype(u32)
    z, core = leaf_id // 2, leaf_id % 2
    node, z8 = z // half, z % half

    plane = [[(2 * k + c) * n_front + f for c in range(2) for f in range(n_front)] for k in range(n_z)]
    z_all = [[2 * k + c for k in range(n_z)] for c in range(2)]
    mid = half // 2
    order = [mid] + [k for k in range(half) if k != mid]
    z_half = [[2 * (h * half + k) + c for k in order] for h in range(2) for c in range(2)]
    swap = [(k, k ^ 1) for k in range(n_leaf)]

    def a2a_plane(v):
        return lax.all_to_all(v, ("leaf", "front"), 0, 0, axis_index_groups=plane)

    def a2a_leaf(v, groups):
        return lax.all_to_all(v, "leaf", 0, 0, axis_index_groups=groups)

    def place(k):
        return jnp.where(k == mid, u32(0), jnp.where(k < mid, k + 1, k))

    def spread(v, n):
        return jnp.broadcast_to(v[None], (n,) + v.shape)

    def by_core(v):
        return jnp.broadcast_to(v[:, None], (2, n_front) + v.shape[1:]).reshape((n_plane,) + v.shape[1:])

    def cut(v):
        v = v.reshape(n_front, PIECE, v.shape[-1])
        return jnp.concatenate([v[:, :WIN], v[:, LO:]], 0)

    def join(v):
        low, high = v[:n_front], v[n_front:, WIN - LO :]
        return jnp.concatenate([low, high], 1).reshape(n_front * PIECE, v.shape[-1])

    def fold(v):
        return v[:n_front].astype(f32) + v[n_front:].astype(f32)

    def total(v):
        return jnp.sum(v.astype(f32), 0)

    def pick(v, k, n):
        return lax.dynamic_slice(v, (k,) + (u32(0),) * (v.ndim - 1), (n,) + v.shape[1:])

    def masked(v, keep):
        return jnp.where(keep[..., None], v, 0.0).astype(bf)

    def dot(a, b):
        return jnp.dot(a, b, preferred_element_type=f32)

    def panel(mat, h, first, last):
        return mat.reshape(2 * height, mat.shape[-1])[h * height : (h + 1) * height, first:last]

    live_a, live_b, live_root = (live[k].reshape(()) * BLK for k in ((0, slice(0, 1)), (0, slice(1, 2)), (1, slice(0, 1))))
    live_node = jnp.where(node == 0, live_a, live_b)
    here = (front_id * PIECE + core * LO).astype(i32)
    at_out = (front_id * sep_dev + (core * half + place(z8)) * PIECE).astype(i32)
    kind = lax.iota(i32, 8)
    count = jnp.where(kind == 2, live_a, jnp.where(kind == 3, live_b, jnp.where((kind < 4) | (kind > 6), live_node, live_root)))
    block = jnp.where((kind > 1) & (kind < 5), z.astype(i32), 2 * z8.astype(i32) + ((kind == 1) | (kind == 6)).astype(i32))
    begin = jnp.where(kind == 7, at_out, here + block * sep_dev)
    keep = lax.broadcasted_iota(i32, (8, PIECE), 1) < (count - begin)[:, None]
    keep = (keep[0:2, :WIN], keep[2, :WIN], keep[3, :WIN], keep[4, :WIN], keep[5:7, :WIN], keep[7])
    scalars = (keep, core, 1 - core, 2 * z8, place(front_id // 2), core == front_id % 2)

    got = a2a_plane(cut(forcing[0]))
    uinv1 = cut(upper_inv[0, :, w0:])
    extra = jnp.concatenate([cut(lower_inv[0, :, w0:]), uinv1[:, :, head:]], 2)
    got, extra, uinv1, scalars = lax.optimization_barrier((got, extra, uinv1[:, :, :head], scalars))
    keep, core, other_core, two_z8, source, mine = scalars

    pair = fold(got).astype(bf).reshape(half, 2 * WIN, n_rhs)
    pair = jnp.concatenate([pair[mid : mid + 1], pair[:mid], pair[mid + 1 :]], 0)
    r0 = total(a2a_leaf(pair, z_half)).reshape(2, WIN, n_rhs)
    moved = a2a_plane(jnp.concatenate([by_core(masked(r0, keep[0])), extra], 2))
    rm0 = join(moved[:, :, :n_rhs])

    c_part = dot(lower_upd[0], rm0).astype(bf)
    y_part = dot(lower_inv[0, :, :w0], rm0).astype(bf)
    parts = fold(a2a_plane(cut(jnp.concatenate([c_part, y_part], 1)))).astype(bf)

    got = a2a_leaf(jnp.concatenate([parts[:, :, :n_rhs], parts[:, :, n_rhs:]], 1), z_all)
    r1 = masked(-total(got[:, :WIN]), keep[3])
    y0 = jnp.stack([masked(total(got[:half, WIN:]), keep[1]), masked(total(got[half:, WIN:]), keep[2])])
    y0 = jnp.broadcast_to(y0[:, None], (2, half, WIN, n_rhs)).reshape(n_z, WIN, n_rhs)
    r1, y0 = lax.optimization_barrier((spread(r1, n_plane), y0))
    r1 = join(a2a_plane(r1))

    blank = jnp.zeros((n_rhs - tail, n_rhs), bf)
    y1 = sum(
        dot(panel(moved, h, n_rhs, n_rhs + w1 + tail), jnp.concatenate([r1[h * w1 : (h + 1) * w1], blank], 0))
        for h in range(2)
    )
    got = a2a_leaf(jnp.concatenate([y1.astype(bf).reshape(n_front, WIN, n_rhs), y0], 1), z_all)
    y1 = masked(total(got[:, :WIN]), keep[3])
    y0 = pick(got[:, WIN:], two_z8, 2)
    got = a2a_plane(jnp.concatenate([spread(y1, n_plane), by_core(y0), uinv1], 2))
    y1 = join(got[:, :, :n_rhs])
    y0 = join(got[:, :, n_rhs : 2 * n_rhs])

    x1 = 0.0
    for h in range(2):
        v = y1[h * w1 : (h + 1) * w1]
        x1 = x1 + dot(panel(got, h, 2 * n_rhs, 2 * n_rhs + head), v[:head])
        x1 = x1 + dot(panel(moved, h, n_rhs + head, n_rhs + head + n_rhs), jnp.concatenate([blank, v[head:]], 0))
    x1 = x1.astype(bf).reshape(half, 2 * WIN, n_rhs)
    x1, y0 = lax.optimization_barrier((jnp.concatenate([x1, x1], 0), y0))
    x1 = masked(total(a2a_leaf(x1, z_all)).reshape(2, WIN, n_rhs), keep[4])
    x1, y0 = lax.optimization_barrier((a2a_plane(by_core(x1)), y0))
    x1 = join(x1)

    term = (dot(upper_inv[0, :, :w0], y0) - dot(upper_upd[0], x1)).reshape(2, half, PIECE, n_rhs)
    x1 = x1.reshape(2, half, PIECE, n_rhs)
    away = jnp.concatenate([pick(term, other_core, 1)[0].astype(bf), pick(x1, other_core, 1)[0]], 1)
    away = lax.ppermute(away, "leaf", swap)
    term = (pick(term, core, 1)[0] + away[:, :PIECE].astype(f32)).astype(bf)
    own = jnp.where(mine, pick(x1, core, 1)[0], away[:, PIECE:])
    got = a2a_leaf(jnp.concatenate([term, own], 1), z_half)

    x0 = masked(total(got[:, :PIECE]), keep[5])
    x1 = pick(got[:, PIECE:], source, 1)[0]
    both = a2a_leaf(spread(jnp.stack([x0, x1]), half), z_half)
    both = jnp.swapaxes(both, 0, 1).reshape(2, half * PIECE, n_rhs)
    other = lax.ppermute(both, "leaf", swap)
    both = jnp.where(core == 0, jnp.concatenate([both, other], 1), jnp.concatenate([other, both], 1))
    return both[:, None]


def solution(mesh):
    return jax.shard_map(
        body,
        mesh=mesh,
        in_specs=(
            P("leaf", "front", None),
            P(),
            P("leaf", "front", None),
            P("leaf", "front", None),
            P("leaf", "front", None),
            P("leaf", "front", None),
        ),
        out_specs=P(None, "leaf", "front", None),
        check_vma=False,
    )
```

```python
import jax
import jax.numpy as jnp
from jax import lax
from jax.sharding import PartitionSpec as P

BLK = 128
WIN = 24
PIECE = 40
LO = PIECE - WIN


def body(forcing, live, lower_inv, lower_upd, upper_inv, upper_upd):
    n_leaf = lax.axis_size("leaf")
    n_front = lax.axis_size("front")
    n_z = n_leaf // 2
    half = n_z // 2
    sep_dev, n_rhs = forcing.shape[1:]
    w0, w1 = sep_dev, sep_dev // 2
    n_plane = 2 * n_front
    height = n_front * WIN
    tail = w1 % n_rhs
    head = w1 - tail
    bf, f32, i32, u32 = jnp.bfloat16, jnp.float32, jnp.int32, jnp.uint32
    leaf_id = lax.axis_index("leaf").astype(u32)
    front_id = lax.axis_index("front").astype(u32)
    z, core = leaf_id // 2, leaf_id % 2
    node, z8 = z // half, z % half

    plane = [[(2 * k + c) * n_front + f for c in (1, 0) for f in range(n_front)] for k in range(n_z)]
    z_all = [[2 * k + c for k in range(n_z)] for c in range(2)]
    mid = half // 2
    order = [mid] + [k for k in range(half) if k != mid]
    z_half = [[2 * (h * half + k) + c for k in order] for h in range(2) for c in range(2)]
    swap = [(k, k ^ 1) for k in range(n_leaf)]

    def a2a_plane(v):
        return lax.all_to_all(v, ("leaf", "front"), 0, 0, axis_index_groups=plane)

    def a2a_leaf(v, groups):
        return lax.all_to_all(v, "leaf", 0, 0, axis_index_groups=groups)

    def place(k):
        return jnp.where(k == mid, u32(0), jnp.where(k < mid, k + 1, k))

    def spread(v, n):
        return jnp.broadcast_to(v[None], (n,) + v.shape)

    def by_core(even, odd):
        v = jnp.stack([odd, even])
        return jnp.broadcast_to(v[:, None], (2, n_front) + v.shape[1:]).reshape((n_plane,) + v.shape[1:])

    def cut(v):
        v = v.reshape(n_front, PIECE, v.shape[-1])
        return jnp.concatenate([v[:, :WIN], v[:, LO:]], 0)

    def join(v):
        low, high = v[:n_front], v[n_front:, WIN - LO :]
        return jnp.concatenate([low, high], 1).reshape(n_front * PIECE, v.shape[-1])

    def join_second(v):
        low, high = v[:n_front, :LO], v[n_front:]
        return jnp.concatenate([low, high], 1).reshape(n_front * PIECE, v.shape[-1])

    def pack(a, b, low):
        first = jnp.concatenate([a, b[..., :LO, :]], -2)
        return jnp.where(low, first, jnp.concatenate([a[..., WIN - LO :, :], b], -2))

    def unpack(v, low):
        return jnp.where(low, v[..., :WIN, :], jnp.concatenate([v[..., : WIN - LO, :], v[..., :LO, :]], -2))

    def unpack_second(v, low):
        first = jnp.concatenate([v[..., WIN:, :], v[..., LO:WIN, :]], -2)
        return jnp.where(low, first, v[..., LO:, :])

    def fold(v):
        return v[:n_front].astype(f32) + v[n_front:].astype(f32)

    def total(v):
        return jnp.sum(v.astype(f32), 0)

    def pick(v, k, n):
        return lax.dynamic_slice(v, (k,) + (u32(0),) * (v.ndim - 1), (n,) + v.shape[1:])

    def masked(v, keep):
        return jnp.where(keep[..., None], v, 0.0).astype(bf)

    def dot(a, b):
        return jnp.dot(a, b, preferred_element_type=f32)

    def panel(mat, h, first, last):
        return mat.reshape(2 * height, mat.shape[-1])[h * height : (h + 1) * height, first:last]

    live_a, live_b, live_root = (live[k].reshape(()) * BLK for k in ((0, slice(0, 1)), (0, slice(1, 2)), (1, slice(0, 1))))
    live_node = jnp.where(node == 0, live_a, live_b)
    here = (front_id * PIECE + (1 - core) * LO).astype(i32)
    at_out = (front_id * sep_dev + (core * half + place(z8)) * PIECE).astype(i32)
    kind = lax.iota(i32, 8)
    count = jnp.where(kind == 2, live_a, jnp.where(kind == 3, live_b, jnp.where((kind < 4) | (kind > 6), live_node, live_root)))
    block = jnp.where((kind > 1) & (kind < 5), z.astype(i32), 2 * z8.astype(i32) + ((kind == 1) | (kind == 6)).astype(i32))
    begin = jnp.where(kind == 7, at_out, here + block * sep_dev)
    keep = lax.broadcasted_iota(i32, (8, PIECE), 1) < (count - begin)[:, None]
    keep = tuple(keep[k, :WIN] for k in range(7)) + (keep[7],)
    scalars = (keep, core, 1 - core, 2 * z8, place(front_id // 2), core == front_id % 2, core == 1)

    got = a2a_plane(cut(forcing[0]))
    uinv1 = cut(upper_inv[0, :, w0:])
    extra = jnp.concatenate([cut(lower_inv[0, :, w0:]), uinv1[:, :, head:]], 2)
    got, extra, uinv1, scalars = lax.optimization_barrier((got, extra, uinv1[:, :, :head], scalars))
    keep, core, other_core, two_z8, source, mine, low = scalars

    pair = fold(got).astype(bf).reshape(half, 2, WIN, n_rhs)
    pair = pack(pair[:, 0], pair[:, 1], low)
    pair = jnp.concatenate([pair[mid : mid + 1], pair[:mid], pair[mid + 1 :]], 0)
    r0 = total(a2a_leaf(pair, z_half))
    rm0 = by_core(masked(unpack(r0, low), keep[0]), masked(unpack_second(r0, low), keep[1]))
    moved = a2a_plane(jnp.concatenate([rm0, extra], 2))
    rm0 = moved[:, :, :n_rhs]
    rm0 = jnp.where(low, join_second(rm0), join(rm0))

    c_part = dot(lower_upd[0], rm0).astype(bf)
    y_part = dot(lower_inv[0, :, :w0], rm0).astype(bf)
    parts = fold(a2a_plane(cut(jnp.concatenate([c_part, y_part], 1)))).astype(bf)

    got = a2a_leaf(pack(parts[:, :, :n_rhs], parts[:, :, n_rhs:], low), z_all)
    sum_a, sum_b = total(got[:half]), total(got[half:])
    r1 = masked(-unpack(sum_a + sum_b, low), keep[4])
    y0 = jnp.stack([masked(unpack_second(sum_a, low), keep[2]), masked(unpack_second(sum_b, low), keep[3])])
    y0 = jnp.broadcast_to(y0[:, None], (2, half, WIN, n_rhs)).reshape(n_z, WIN, n_rhs)
    r1, y0 = lax.optimization_barrier((spread(r1, n_plane), y0))
    r1 = join(a2a_plane(r1))

    blank = jnp.zeros((n_rhs - tail, n_rhs), bf)
    y1 = sum(
        dot(panel(moved, h, n_rhs, n_rhs + w1 + tail), jnp.concatenate([r1[(1 - h) * w1 : (2 - h) * w1], blank], 0))
        for h in range(2)
    )
    got = a2a_leaf(pack(y1.astype(bf).reshape(n_front, WIN, n_rhs), y0, low), z_all)
    y1 = masked(unpack(total(got), low), keep[4])
    y0 = unpack_second(pick(got, two_z8, 2), low)
    got = a2a_plane(jnp.concatenate([spread(y1, n_plane), by_core(y0[0], y0[1]), uinv1], 2))
    y1 = join(got[:, :, :n_rhs])
    y0 = join_second(got[:, :, n_rhs : 2 * n_rhs])

    x1 = 0.0
    for h in range(2):
        v = y1[(1 - h) * w1 : (2 - h) * w1]
        x1 = x1 + dot(panel(got, h, 2 * n_rhs, 2 * n_rhs + head), v[:head])
        x1 = x1 + dot(panel(moved, h, n_rhs + head, n_rhs + head + n_rhs), jnp.concatenate([blank, v[head:]], 0))
    x1 = x1.astype(bf).reshape(half, 2, WIN, n_rhs)
    x1 = pack(x1[:, 0], x1[:, 1], low)
    x1, y0 = lax.optimization_barrier((jnp.concatenate([x1, x1], 0), y0))
    x1 = total(a2a_leaf(x1, z_all))
    x1 = by_core(masked(unpack(x1, low), keep[5]), masked(unpack_second(x1, low), keep[6]))
    x1, y0 = lax.optimization_barrier((a2a_plane(x1), y0))
    x1 = jnp.where(low, join_second(x1), join(x1))

    term = (dot(upper_inv[0, :, :w0], y0) - dot(upper_upd[0], x1)).reshape(2, half, PIECE, n_rhs)
    x1 = x1.reshape(2, half, PIECE, n_rhs)
    away = jnp.concatenate([pick(term, other_core, 1)[0].astype(bf), pick(x1, other_core, 1)[0]], 1)
    away = lax.ppermute(away, "leaf", swap)
    term = (pick(term, core, 1)[0] + away[:, :PIECE].astype(f32)).astype(bf)
    own = jnp.where(mine, pick(x1, core, 1)[0], away[:, PIECE:])
    got = a2a_leaf(jnp.concatenate([term, own], 1), z_half)

    x0 = masked(total(got[:, :PIECE]), keep[7])
    x1 = pick(got[:, PIECE:], source, 1)[0]
    both = a2a_leaf(spread(jnp.stack([x0, x1]), half), z_half)
    both = jnp.swapaxes(both, 0, 1).reshape(2, half * PIECE, n_rhs)
    other = lax.ppermute(both, "leaf", swap)
    both = jnp.where(core == 0, jnp.concatenate([both, other], 1), jnp.concatenate([other, both], 1))
    return both[:, None]


def solution(mesh):
    return jax.shard_map(
        body,
        mesh=mesh,
        in_specs=(
            P("leaf", "front", None),
            P(),
            P("leaf", "front", None),
            P("leaf", "front", None),
            P("leaf", "front", None),
            P("leaf", "front", None),
        ),
        out_specs=P(None, "leaf", "front", None),
        check_vma=False,
    )
```

```python
import jax
import jax.numpy as jnp
import numpy as np
from jax import lax
from jax.sharding import PartitionSpec as P

BLK = 128
WIN = 24
PIECE = 40
LO = PIECE - WIN


def body(forcing, live, lower_inv, lower_upd, upper_inv, upper_upd):
    n_leaf = lax.axis_size("leaf")
    n_front = lax.axis_size("front")
    n_z = n_leaf // 2
    half = n_z // 2
    sep_dev, n_rhs = forcing.shape[1:]
    w0, w1 = sep_dev, sep_dev // 2
    n_plane = 2 * n_front
    height = n_front * WIN
    tail = w1 % n_rhs
    head = w1 - tail
    bf, f32, i32, u32 = jnp.bfloat16, jnp.float32, jnp.int32, jnp.uint32
    leaf_id = lax.axis_index("leaf").astype(u32)
    front_id = lax.axis_index("front").astype(u32)
    z, core = leaf_id // 2, leaf_id % 2
    node, z8 = z // half, z % half

    shift = half - 2
    turn = shift // 2
    fronts = [(k + shift) % n_front for k in range(n_front)]
    planes = [(k + shift) % n_z for k in range(n_z)]
    halves = [(k + turn) % half for k in range(half)]
    plane = [[(2 * k + c) * n_front + f for c in (1, 0) for f in fronts] for k in range(n_z)]
    z_all = [[2 * k + c for k in planes] for c in range(2)]
    z_half = [[2 * (h * half + k) + c for k in halves] for h in range(2) for c in range(2)]
    swap = [(k, k ^ 1) for k in range(n_leaf)]

    def a2a_plane(v):
        return lax.all_to_all(v, ("leaf", "front"), 0, 0, axis_index_groups=plane)

    def a2a_leaf(v, groups):
        return lax.all_to_all(v, "leaf", 0, 0, axis_index_groups=groups)

    def place(k):
        return (k + (half - turn)) % half

    def spread(v, n):
        return jnp.broadcast_to(v[None], (n,) + v.shape)

    def by_core(even, odd):
        v = jnp.stack([odd, even])
        return jnp.broadcast_to(v[:, None], (2, n_front) + v.shape[1:]).reshape((n_plane,) + v.shape[1:])

    def cut(v):
        v = v.reshape(n_front, PIECE, v.shape[-1])
        return jnp.concatenate([v[:, :WIN], v[:, LO:]], 0)

    def join(v):
        low, high = v[:n_front], v[n_front:, WIN - LO :]
        return jnp.concatenate([low, high], 1).reshape(n_front * PIECE, v.shape[-1])

    def join_second(v):
        low, high = v[:n_front, :LO], v[n_front:]
        return jnp.concatenate([low, high], 1).reshape(n_front * PIECE, v.shape[-1])

    def lift(a, low):
        blank = jnp.zeros(a.shape[:-2] + (LO, n_rhs), a.dtype)
        first = jnp.concatenate([a, blank], -2)
        return jnp.where(low, first, jnp.concatenate([a[..., WIN - LO :, :], blank, blank[..., : WIN - LO, :]], -2))

    def lift_second(b, low):
        blank = jnp.zeros(b.shape[:-2] + (LO, n_rhs), b.dtype)
        first = jnp.concatenate([blank, blank[..., : WIN - LO, :], b[..., :LO, :]], -2)
        return jnp.where(low, first, jnp.concatenate([blank, b], -2))

    def pack(a, b, low):
        first = jnp.concatenate([a, b[..., :LO, :]], -2)
        return jnp.where(low, first, jnp.concatenate([a[..., WIN - LO :, :], b], -2))

    def unpack(v, low):
        return jnp.where(low, v[..., :WIN, :], jnp.concatenate([v[..., : WIN - LO, :], v[..., :LO, :]], -2))

    def unpack_second(v, low):
        first = jnp.concatenate([v[..., WIN:, :], v[..., LO:WIN, :]], -2)
        return jnp.where(low, first, v[..., LO:, :])

    def fold(v):
        return v[:n_front].astype(f32) + v[n_front:].astype(f32)

    def total(v):
        return jnp.sum(v.astype(f32), 0)

    def pick(v, k, n):
        return lax.dynamic_slice(v, (k,) + (np.uint32(0),) * (v.ndim - 1), (n,) + v.shape[1:])

    def masked(v, keep):
        return jnp.where(keep[..., None], v, 0.0).astype(bf)

    def dot(a, b):
        return jnp.dot(a, b, preferred_element_type=f32)

    def panel(mat, h, first, last):
        return mat.reshape(2 * height, mat.shape[-1])[h * height : (h + 1) * height, first:last]

    live_a, live_b, live_root = (live[k].reshape(()) * BLK for k in ((0, slice(0, 1)), (0, slice(1, 2)), (1, slice(0, 1))))
    live_node = jnp.where(node == 0, live_a, live_b)
    here = ((front_id + (n_front - shift)) % n_front * PIECE + (1 - core) * LO).astype(i32)
    at_out = (front_id * sep_dev + (core * half + place(z8)) * PIECE).astype(i32)
    kind = lax.iota(i32, 8)
    count = jnp.where(kind == 2, live_a, jnp.where(kind == 3, live_b, jnp.where((kind < 4) | (kind > 6), live_node, live_root)))
    block = jnp.where((kind > 1) & (kind < 5), z.astype(i32), 2 * z8.astype(i32) + ((kind == 1) | (kind == 6)).astype(i32))
    begin = jnp.where(kind == 7, at_out, here + block * sep_dev)
    keep = lax.broadcasted_iota(i32, (8, PIECE), 1) < (count - begin)[:, None]
    keep = tuple(keep[k, :WIN] for k in range(7)) + (keep[7],)
    scalars = (keep, core, 1 - core, (2 * z8 + (n_z - shift)) % n_z, place(front_id // 2), core == front_id % 2, core == 1)

    got = a2a_plane(cut(forcing[0]))
    uinv1 = cut(upper_inv[0, :, w0:])
    extra = jnp.concatenate([cut(lower_inv[0, :, w0:]), uinv1[:, :, head:]], 2)
    got, extra, uinv1, scalars = lax.optimization_barrier((got, extra, uinv1[:, :, :head], scalars))
    keep, core, other_core, two_z8, source, mine, low = scalars

    pair = fold(got).astype(bf).reshape(half, 2, WIN, n_rhs)
    pair = pack(pair[:, 0], pair[:, 1], low)
    r0 = total(a2a_leaf(pair, z_half))
    rm0 = by_core(masked(unpack(r0, low), keep[0]), masked(unpack_second(r0, low), keep[1]))
    moved = a2a_plane(jnp.concatenate([rm0, extra], 2))
    rm0 = moved[:, :, :n_rhs]
    rm0 = jnp.where(low, join_second(rm0), join(rm0))

    c_part = dot(lower_upd[0], rm0).astype(bf)
    y_part = dot(lower_inv[0, :, :w0], rm0).astype(bf)
    parts = fold(a2a_plane(cut(jnp.concatenate([c_part, y_part], 1)))).astype(bf)

    got = a2a_leaf(pack(parts[:, :, :n_rhs], parts[:, :, n_rhs:], low), z_all)
    edge = half - shift
    sum_a, sum_b = total(got[:edge]) + total(got[edge + half :]), total(got[edge : edge + half])
    r1 = masked(-unpack(sum_a + sum_b, low), keep[4])
    y0_a, y0_b = masked(unpack_second(sum_a, low), keep[2]), masked(unpack_second(sum_b, low), keep[3])
    y0 = jnp.concatenate([spread(y0_a, edge), spread(y0_b, half), spread(y0_a, shift)], 0)
    r1, y0 = lax.optimization_barrier((spread(r1, n_plane), lift_second(y0, low)))
    r1 = join(a2a_plane(r1))

    blank = jnp.zeros((n_rhs - tail, n_rhs), bf)
    y1 = sum(
        dot(panel(moved, h, n_rhs, n_rhs + w1 + tail), jnp.concatenate([r1[(1 - h) * w1 : (2 - h) * w1], blank], 0))
        for h in range(2)
    )
    got = a2a_leaf(lift(y1.astype(bf).reshape(n_front, WIN, n_rhs), low) + y0, z_all)
    y1 = masked(unpack(total(got), low), keep[4])
    y0 = unpack_second(lax.optimization_barrier(pick(got, two_z8, 2)), low)
    got = a2a_plane(jnp.concatenate([spread(y1, n_plane), by_core(y0[0], y0[1]), uinv1], 2))
    y1 = join(got[:, :, :n_rhs])
    y0 = join_second(got[:, :, n_rhs : 2 * n_rhs])

    x1 = 0.0
    for h in range(2):
        v = y1[(1 - h) * w1 : (2 - h) * w1]
        x1 = x1 + dot(panel(got, h, 2 * n_rhs, 2 * n_rhs + head), v[:head])
        x1 = x1 + dot(panel(moved, h, n_rhs + head, n_rhs + head + n_rhs), jnp.concatenate([blank, v[head:]], 0))
    x1 = x1.astype(bf).reshape(half, 2, WIN, n_rhs)
    x1 = pack(x1[:, 0], x1[:, 1], low)
    x1, y0 = lax.optimization_barrier((jnp.concatenate([x1[turn:], x1, x1[:turn]], 0), y0))
    x1 = total(a2a_leaf(x1, z_all))
    x1 = by_core(masked(unpack(x1, low), keep[5]), masked(unpack_second(x1, low), keep[6]))
    x1, y0 = lax.optimization_barrier((a2a_plane(x1), y0))
    x1 = jnp.where(low, join_second(x1), join(x1))

    term = (dot(upper_inv[0, :, :w0], y0) - dot(upper_upd[0], x1)).reshape(2, half, PIECE, n_rhs)
    x1 = x1.reshape(2, half, PIECE, n_rhs)
    away = jnp.concatenate([pick(term, other_core, 1)[0].astype(bf), pick(x1, other_core, 1)[0]], 1)
    away = lax.ppermute(away, "leaf", swap)
    term = (pick(term, core, 1)[0] + away[:, :PIECE].astype(f32)).astype(bf)
    own = jnp.where(mine, pick(x1, core, 1)[0], away[:, PIECE:])
    got = a2a_leaf(jnp.concatenate([term, own], 1), z_half)

    x0 = masked(total(got[:, :PIECE]), keep[7])
    x1 = pick(got[:, PIECE:], source, 1)[0]
    both = a2a_leaf(spread(jnp.stack([x0, x1]), half), z_half)
    both = jnp.swapaxes(both, 0, 1).reshape(2, half * PIECE, n_rhs)
    other = lax.ppermute(both, "leaf", swap)
    both = jnp.where(core == 0, jnp.concatenate([both, other], 1), jnp.concatenate([other, both], 1))
    return both[:, None]


def solution(mesh):
    return jax.shard_map(
        body,
        mesh=mesh,
        in_specs=(
            P("leaf", "front", None),
            P(),
            P("leaf", "front", None),
            P("leaf", "front", None),
            P("leaf", "front", None),
            P("leaf", "front", None),
        ),
        out_specs=P(None, "leaf", "front", None),
        check_vma=False,
    )
```

```python
import jax
import jax.numpy as jnp
import numpy as np
from jax import lax
from jax.sharding import PartitionSpec as P

BLK = 128
WIN = 24
PIECE = 40
LO = PIECE - WIN


def body(forcing, live, lower_inv, lower_upd, upper_inv, upper_upd):
    n_leaf = lax.axis_size("leaf")
    n_front = lax.axis_size("front")
    n_z = n_leaf // 2
    half = n_z // 2
    sep_dev, n_rhs = forcing.shape[1:]
    w0, w1 = sep_dev, sep_dev // 2
    n_plane = 2 * n_front
    height = n_front * WIN
    tail = w1 % n_rhs
    head = w1 - tail
    bf, f32, i32, u32 = jnp.bfloat16, jnp.float32, jnp.int32, jnp.uint32
    leaf_id = lax.axis_index("leaf").astype(u32)
    front_id = lax.axis_index("front").astype(u32)
    z, core = leaf_id // 2, leaf_id % 2
    node, z8 = z // half, z % half

    shift = half - 2
    turn = shift // 2
    fronts = [(k + shift) % n_front for k in range(n_front)]
    planes = [(k + shift) % n_z for k in range(n_z)]
    halves = [(k + turn) % half for k in range(half)]
    plane = [[(2 * k + c) * n_front + f for c in (1, 0) for f in fronts] for k in range(n_z)]
    z_all = [[2 * k + c for k in planes] for c in range(2)]
    z_half = [[2 * (h * half + k) + c for k in halves] for h in range(2) for c in range(2)]
    mid = half // 2
    middle_first = [mid] + [k for k in range(half) if k != mid]
    z_last = [[2 * (h * half + k) + c for k in middle_first] for h in range(2) for c in range(2)]
    swap = [(k, k ^ 1) for k in range(n_leaf)]

    def a2a_plane(v):
        return lax.all_to_all(v, ("leaf", "front"), 0, 0, axis_index_groups=plane)

    def a2a_leaf(v, groups):
        return lax.all_to_all(v, "leaf", 0, 0, axis_index_groups=groups)

    def place(k):
        return jnp.where(k == mid, u32(0), jnp.where(k < mid, k + 1, k))

    def spread(v, n):
        return jnp.broadcast_to(v[None], (n,) + v.shape)

    def by_core(even, odd):
        v = jnp.stack([odd, even])
        return jnp.broadcast_to(v[:, None], (2, n_front) + v.shape[1:]).reshape((n_plane,) + v.shape[1:])

    def cut(v):
        v = v.reshape(n_front, PIECE, v.shape[-1])
        return jnp.concatenate([v[:, :WIN], v[:, LO:]], 0)

    def join(v):
        low, high = v[:n_front], v[n_front:, WIN - LO :]
        return jnp.concatenate([low, high], 1).reshape(n_front * PIECE, v.shape[-1])

    def join_second(v):
        low, high = v[:n_front, :LO], v[n_front:]
        return jnp.concatenate([low, high], 1).reshape(n_front * PIECE, v.shape[-1])

    def lift(a, low):
        blank = jnp.zeros(a.shape[:-2] + (LO, n_rhs), a.dtype)
        first = jnp.concatenate([a, blank], -2)
        return jnp.where(low, first, jnp.concatenate([a[..., WIN - LO :, :], blank, blank[..., : WIN - LO, :]], -2))

    def lift_second(b, low):
        blank = jnp.zeros(b.shape[:-2] + (LO, n_rhs), b.dtype)
        first = jnp.concatenate([blank, blank[..., : WIN - LO, :], b[..., :LO, :]], -2)
        return jnp.where(low, first, jnp.concatenate([blank, b], -2))

    def pack(a, b, low):
        first = jnp.concatenate([a, b[..., :LO, :]], -2)
        return jnp.where(low, first, jnp.concatenate([a[..., WIN - LO :, :], b], -2))

    def unpack(v, low):
        return jnp.where(low, v[..., :WIN, :], jnp.concatenate([v[..., : WIN - LO, :], v[..., :LO, :]], -2))

    def unpack_second(v, low):
        first = jnp.concatenate([v[..., WIN:, :], v[..., LO:WIN, :]], -2)
        return jnp.where(low, first, v[..., LO:, :])

    def fold(v):
        return v[:n_front].astype(f32) + v[n_front:].astype(f32)

    def total(v):
        return jnp.sum(v.astype(f32), 0)

    def pick(v, k, n):
        return lax.dynamic_slice(v, (k,) + (np.uint32(0),) * (v.ndim - 1), (n,) + v.shape[1:])

    def masked(v, keep):
        return jnp.where(keep[..., None], v, 0.0).astype(bf)

    def dot(a, b):
        return jnp.dot(a, b, preferred_element_type=f32)

    def panel(mat, h, first, last):
        return mat.reshape(2 * height, mat.shape[-1])[h * height : (h + 1) * height, first:last]

    live_a, live_b, live_root = (live[k].reshape(()) * BLK for k in ((0, slice(0, 1)), (0, slice(1, 2)), (1, slice(0, 1))))
    live_node = jnp.where(node == 0, live_a, live_b)
    here = ((front_id + (n_front - shift)) % n_front * PIECE + (1 - core) * LO).astype(i32)
    at_out = (front_id * sep_dev + (core * half + place(z8)) * PIECE).astype(i32)
    kind = lax.iota(i32, 8)
    count = jnp.where(kind == 2, live_a, jnp.where(kind == 3, live_b, jnp.where((kind < 4) | (kind > 6), live_node, live_root)))
    block = jnp.where((kind > 1) & (kind < 5), z.astype(i32), 2 * z8.astype(i32) + ((kind == 1) | (kind == 6)).astype(i32))
    begin = jnp.where(kind == 7, at_out, here + block * sep_dev)
    keep = lax.broadcasted_iota(i32, (8, PIECE), 1) < (count - begin)[:, None]
    keep = tuple(keep[k, :WIN] for k in range(7)) + (keep[7],)
    scalars = (keep, core, 1 - core, (2 * z8 + (n_z - shift)) % n_z, place(front_id // 2), core == front_id % 2, core == 1)

    got = a2a_plane(cut(forcing[0]))
    uinv1 = cut(upper_inv[0, :, w0:])
    extra = jnp.concatenate([cut(lower_inv[0, :, w0:]), uinv1[:, :, head:]], 2)
    got, extra, uinv1, scalars = lax.optimization_barrier((got, extra, uinv1[:, :, :head], scalars))
    keep, core, other_core, two_z8, source, mine, low = scalars

    pair = fold(got).astype(bf).reshape(half, 2, WIN, n_rhs)
    pair = pack(pair[:, 0], pair[:, 1], low)
    r0 = total(a2a_leaf(pair, z_half))
    rm0 = by_core(masked(unpack(r0, low), keep[0]), masked(unpack_second(r0, low), keep[1]))
    moved = a2a_plane(jnp.concatenate([rm0, extra], 2))
    rm0 = moved[:, :, :n_rhs]
    rm0 = jnp.where(low, join_second(rm0), join(rm0))

    c_part = dot(lower_upd[0], rm0).astype(bf).reshape(n_front, PIECE, n_rhs)
    y_part = dot(lower_inv[0, :, :w0], rm0).astype(bf).reshape(n_front, PIECE, n_rhs)
    parts = jnp.stack(
        [
            jnp.concatenate([c_part[:, :WIN], y_part[:, :LO]], 1),
            jnp.concatenate([c_part[:, WIN:], y_part[:, LO:]], 1),
        ]
    )
    parts = fold(a2a_plane(parts.reshape(n_plane, PIECE, n_rhs))).astype(bf)

    got = a2a_leaf(parts, z_all)
    edge = half - shift
    sum_a, sum_b = total(got[:edge]) + total(got[edge + half :]), total(got[edge : edge + half])
    r1 = masked(-unpack(sum_a + sum_b, low), keep[4])
    y0_a, y0_b = masked(unpack_second(sum_a, low), keep[2]), masked(unpack_second(sum_b, low), keep[3])
    y0 = jnp.concatenate([spread(y0_a, edge), spread(y0_b, half), spread(y0_a, shift)], 0)
    r1, y0 = lax.optimization_barrier((spread(r1, n_plane), lift_second(y0, low)))
    r1 = join(a2a_plane(r1))

    blank = jnp.zeros((n_rhs - tail, n_rhs), bf)
    y1 = sum(
        dot(panel(moved, h, n_rhs, n_rhs + w1 + tail), jnp.concatenate([r1[(1 - h) * w1 : (2 - h) * w1], blank], 0))
        for h in range(2)
    )
    got = a2a_leaf(lift(y1.astype(bf).reshape(n_front, WIN, n_rhs), low) + y0, z_all)
    y1 = masked(unpack(total(got), low), keep[4])
    y0 = unpack_second(lax.optimization_barrier(pick(got, two_z8, 2)), low)
    got = a2a_plane(jnp.concatenate([spread(y1, n_plane), by_core(y0[0], y0[1]), uinv1], 2))
    y1 = join(got[:, :, :n_rhs])
    y0 = join_second(got[:, :, n_rhs : 2 * n_rhs])

    x1 = 0.0
    for h in range(2):
        v = y1[(1 - h) * w1 : (2 - h) * w1]
        x1 = x1 + dot(panel(got, h, 2 * n_rhs, 2 * n_rhs + head), v[:head])
        x1 = x1 + dot(panel(moved, h, n_rhs + head, n_rhs + head + n_rhs), jnp.concatenate([blank, v[head:]], 0))
    x1 = x1.astype(bf).reshape(half, 2, WIN, n_rhs)
    x1 = pack(x1[:, 0], x1[:, 1], low)
    x1, y0 = lax.optimization_barrier((jnp.concatenate([x1[turn:], x1, x1[:turn]], 0), y0))
    x1 = total(a2a_leaf(x1, z_all))
    x1 = by_core(masked(unpack(x1, low), keep[5]), masked(unpack_second(x1, low), keep[6]))
    x1, y0 = lax.optimization_barrier((a2a_plane(x1), y0))
    x1 = jnp.where(low, join_second(x1), join(x1))

    term = (dot(upper_inv[0, :, :w0], y0) - dot(upper_upd[0], x1)).reshape(2, half, PIECE, n_rhs)
    x1 = x1.reshape(2, half, PIECE, n_rhs)
    away = jnp.concatenate([pick(term, other_core, 1)[0].astype(bf), pick(x1, other_core, 1)[0]], 1)
    away = lax.ppermute(away, "leaf", swap)
    term = (pick(term, core, 1)[0] + away[:, :PIECE].astype(f32)).astype(bf)
    own = jnp.where(mine, pick(x1, core, 1)[0], away[:, PIECE:])
    got = a2a_leaf(jnp.concatenate([term, own], 1), z_last)

    x0 = masked(total(got[:, :PIECE]), keep[7])
    x1 = pick(got[:, PIECE:], source, 1)[0]
    both = a2a_leaf(spread(jnp.stack([x0, x1]), half), z_last)
    both = jnp.swapaxes(both, 0, 1).reshape(2, half * PIECE, n_rhs)
    other = lax.ppermute(both, "leaf", swap)
    both = jnp.where(core == 0, jnp.concatenate([both, other], 1), jnp.concatenate([other, both], 1))
    return both[:, None]


def solution(mesh):
    return jax.shard_map(
        body,
        mesh=mesh,
        in_specs=(
            P("leaf", "front", None),
            P(),
            P("leaf", "front", None),
            P("leaf", "front", None),
            P("leaf", "front", None),
            P("leaf", "front", None),
        ),
        out_specs=P(None, "leaf", "front", None),
        check_vma=False,
    )
```

```python
import jax
import jax.numpy as jnp
import numpy as np
from jax import lax
from jax.sharding import PartitionSpec as P

BLK = 128
WIN = 24
PIECE = 40
LO = PIECE - WIN


def body(forcing, live, lower_inv, lower_upd, upper_inv, upper_upd):
    n_leaf = lax.axis_size("leaf")
    n_front = lax.axis_size("front")
    n_z = n_leaf // 2
    half = n_z // 2
    sep_dev, n_rhs = forcing.shape[1:]
    w0, w1 = sep_dev, sep_dev // 2
    n_plane = 2 * n_front
    height = n_front * WIN
    tail = w1 % n_rhs
    head = w1 - tail
    bf, f32, i32, u32 = jnp.bfloat16, jnp.float32, jnp.int32, jnp.uint32
    leaf_id = lax.axis_index("leaf").astype(u32)
    front_id = lax.axis_index("front").astype(u32)
    z, core = leaf_id // 2, leaf_id % 2
    node, z8 = z // half, z % half

    shift = half - 2
    turn = shift // 2
    fronts = [(k + shift) % n_front for k in range(n_front)]
    planes = [(k + shift) % n_z for k in range(n_z)]
    halves = [(k + turn) % half for k in range(half)]
    plane = [[(2 * k + c) * n_front + f for c in (1, 0) for f in fronts] for k in range(n_z)]
    z_all = [[2 * k + c for k in planes] for c in range(2)]
    z_half = [[2 * (h * half + k) + c for k in halves] for h in range(2) for c in range(2)]
    mid = half // 2
    middle_first = [mid] + [k for k in range(half) if k != mid]
    z_last = [[2 * (h * half + k) + c for k in middle_first] for h in range(2) for c in range(2)]
    swap = [(k, k ^ 1) for k in range(n_leaf)]

    def a2a_plane(v):
        return lax.all_to_all(v, ("leaf", "front"), 0, 0, axis_index_groups=plane)

    def a2a_leaf(v, groups):
        return lax.all_to_all(v, "leaf", 0, 0, axis_index_groups=groups)

    def place(k):
        return jnp.where(k == mid, u32(0), jnp.where(k < mid, k + 1, k))

    def spread(v, n):
        return jnp.broadcast_to(v[None], (n,) + v.shape)

    def by_core(even, odd):
        v = jnp.stack([odd, even])
        return jnp.broadcast_to(v[:, None], (2, n_front) + v.shape[1:]).reshape((n_plane,) + v.shape[1:])

    def cut(v):
        v = v.reshape(n_front, PIECE, v.shape[-1])
        return jnp.concatenate([v[:, :WIN], v[:, LO:]], 0)

    def join(v):
        low, high = v[:n_front], v[n_front:, WIN - LO :]
        return jnp.concatenate([low, high], 1).reshape(n_front * PIECE, v.shape[-1])

    def join_second(v):
        low, high = v[:n_front, :LO], v[n_front:]
        return jnp.concatenate([low, high], 1).reshape(n_front * PIECE, v.shape[-1])

    def lift(a, low):
        blank = jnp.zeros(a.shape[:-2] + (LO, n_rhs), a.dtype)
        first = jnp.concatenate([a, blank], -2)
        return jnp.where(low, first, jnp.concatenate([a[..., WIN - LO :, :], blank, blank[..., : WIN - LO, :]], -2))

    def lift_second(b, low):
        blank = jnp.zeros(b.shape[:-2] + (LO, n_rhs), b.dtype)
        first = jnp.concatenate([blank, blank[..., : WIN - LO, :], b[..., :LO, :]], -2)
        return jnp.where(low, first, jnp.concatenate([blank, b], -2))

    def pack(a, b, low):
        first = jnp.concatenate([a, b[..., :LO, :]], -2)
        return jnp.where(low, first, jnp.concatenate([a[..., WIN - LO :, :], b], -2))

    def unpack(v, low):
        return jnp.where(low, v[..., :WIN, :], jnp.concatenate([v[..., : WIN - LO, :], v[..., :LO, :]], -2))

    def unpack_second(v, low):
        first = jnp.concatenate([v[..., WIN:, :], v[..., LO:WIN, :]], -2)
        return jnp.where(low, first, v[..., LO:, :])

    def fold(v):
        return v[:n_front].astype(f32) + v[n_front:].astype(f32)

    def total(v):
        return jnp.sum(v.astype(f32), 0)

    def pick(v, k, n):
        return lax.dynamic_slice(v, (k,) + (np.uint32(0),) * (v.ndim - 1), (n,) + v.shape[1:])

    def masked(v, keep):
        return jnp.where(keep[..., None], v, 0.0).astype(bf)

    def dot(a, b):
        return jnp.dot(a, b, preferred_element_type=f32)

    def panel(mat, h, first, last):
        return mat.reshape(2 * height, mat.shape[-1])[h * height : (h + 1) * height, first:last]

    live_a, live_b, live_root = (live[k].reshape(()) * BLK for k in ((0, slice(0, 1)), (0, slice(1, 2)), (1, slice(0, 1))))
    live_node = jnp.where(node == 0, live_a, live_b)
    here = ((front_id + (n_front - shift)) % n_front * PIECE + (1 - core) * LO).astype(i32)
    at_out = (front_id * sep_dev + (core * half + place(z8)) * PIECE).astype(i32)
    kind = lax.iota(i32, 8)
    count = jnp.where(kind == 2, live_a, jnp.where(kind == 3, live_b, jnp.where((kind < 4) | (kind > 6), live_node, live_root)))
    block = jnp.where((kind > 1) & (kind < 5), z.astype(i32), 2 * z8.astype(i32) + ((kind == 1) | (kind == 6)).astype(i32))
    begin = jnp.where(kind == 7, at_out, here + block * sep_dev)
    keep = lax.broadcasted_iota(i32, (8, PIECE), 1) < (count - begin)[:, None]
    keep = tuple(keep[k, :WIN] for k in range(7)) + (keep[7],)
    scalars = (keep, core, 1 - core, (2 * z8 + (n_z - shift)) % n_z, place(front_id // 2), core == front_id % 2, core == 1)

    got = a2a_plane(cut(forcing[0]))
    uinv1 = cut(upper_inv[0, :, w0:])
    extra = jnp.concatenate([cut(lower_inv[0, :, w0:]), uinv1[:, :, head:]], 2)
    got, extra, uinv1, scalars = lax.optimization_barrier((got, extra, uinv1[:, :, :head], scalars))
    keep, core, other_core, two_z8, source, mine, low = scalars

    pair = fold(got).astype(bf).reshape(half, 2, WIN, n_rhs)
    pair = pack(pair[:, 0], pair[:, 1], low)
    r0 = total(a2a_leaf(pair, z_half))
    rm0 = by_core(masked(unpack(r0, low), keep[0]), masked(unpack_second(r0, low), keep[1]))
    moved = a2a_plane(jnp.concatenate([rm0, extra], 2))
    rm0 = moved[:, :, :n_rhs]
    rm0 = jnp.where(low, join_second(rm0), join(rm0))

    c_part = dot(lower_upd[0], rm0).astype(bf).reshape(n_front, PIECE, n_rhs)
    y_part = dot(lower_inv[0, :, :w0], rm0).astype(bf).reshape(n_front, PIECE, n_rhs)
    parts = jnp.stack(
        [
            jnp.concatenate([c_part[:, :WIN], y_part[:, :LO]], 1),
            jnp.concatenate([c_part[:, WIN:], y_part[:, LO:]], 1),
        ]
    )
    parts = fold(a2a_plane(parts.reshape(n_plane, PIECE, n_rhs))).astype(bf)

    got = a2a_leaf(parts, z_all)
    edge = half - shift
    sum_a, sum_b = total(got[:edge]) + total(got[edge + half :]), total(got[edge : edge + half])
    r1 = masked(-unpack(sum_a + sum_b, low), keep[4])
    y0_a, y0_b = masked(unpack_second(sum_a, low), keep[2]), masked(unpack_second(sum_b, low), keep[3])
    y0 = jnp.concatenate([spread(y0_a, edge), spread(y0_b, half), spread(y0_a, shift)], 0)
    r1, y0 = lax.optimization_barrier((spread(r1, n_plane), lift_second(y0, low)))
    r1 = join(a2a_plane(r1))

    blank = jnp.zeros((n_rhs - tail, n_rhs), bf)
    y1 = sum(
        dot(panel(moved, h, n_rhs, n_rhs + w1 + tail), jnp.concatenate([r1[(1 - h) * w1 : (2 - h) * w1], blank], 0))
        for h in range(2)
    )
    got = a2a_leaf(lift(y1.astype(bf).reshape(n_front, WIN, n_rhs), low) + y0, z_all)
    y1 = masked(unpack(total(got), low), keep[4])
    y0 = unpack_second(lax.optimization_barrier(pick(got, two_z8, 2)), low)
    got = a2a_plane(jnp.concatenate([spread(y1, n_plane), by_core(y0[0], y0[1]), uinv1], 2))
    y1 = join(got[:, :, :n_rhs])
    y0 = join_second(got[:, :, n_rhs : 2 * n_rhs])

    x1 = 0.0
    for h in range(2):
        v = y1[(1 - h) * w1 : (2 - h) * w1]
        x1 = x1 + dot(panel(got, h, 2 * n_rhs, 2 * n_rhs + head), v[:head])
        x1 = x1 + dot(panel(moved, h, n_rhs + head, n_rhs + head + n_rhs), jnp.concatenate([blank, v[head:]], 0))
    x1 = x1.astype(bf).reshape(half, 2, WIN, n_rhs)
    x1 = pack(x1[:, 0], x1[:, 1], low)
    x1, y0 = lax.optimization_barrier((jnp.concatenate([x1[turn:], x1, x1[:turn]], 0), y0))
    x1, y0 = lax.optimization_barrier((total(a2a_leaf(x1, z_all)), y0))
    x1 = by_core(masked(unpack(x1, low), keep[5]), masked(unpack_second(x1, low), keep[6]))
    x1, term = lax.optimization_barrier((x1, dot(upper_inv[0, :, :w0], y0)))
    x1 = a2a_plane(x1)
    x1 = jnp.where(low, join_second(x1), join(x1))

    term = (term - dot(upper_upd[0], x1)).reshape(2, half, PIECE, n_rhs)
    x1 = x1.reshape(2, half, PIECE, n_rhs)
    away = jnp.concatenate([pick(term, other_core, 1)[0].astype(bf), pick(x1, other_core, 1)[0]], 1)
    away = lax.ppermute(away, "leaf", swap)
    term = (pick(term, core, 1)[0] + away[:, :PIECE].astype(f32)).astype(bf)
    own = jnp.where(mine, pick(x1, core, 1)[0], away[:, PIECE:])
    got = a2a_leaf(jnp.concatenate([term, own], 1), z_last)

    x0 = masked(total(got[:, :PIECE]), keep[7])
    x1 = pick(got[:, PIECE:], source, 1)[0]
    both = a2a_leaf(spread(jnp.stack([x0, x1]), half), z_last)
    both = jnp.swapaxes(both, 0, 1).reshape(2, half * PIECE, n_rhs)
    other = lax.ppermute(both, "leaf", swap)
    both = jnp.where(core == 0, jnp.concatenate([both, other], 1), jnp.concatenate([other, both], 1))
    return both[:, None]


def solution(mesh):
    return jax.shard_map(
        body,
        mesh=mesh,
        in_specs=(
            P("leaf", "front", None),
            P(),
            P("leaf", "front", None),
            P("leaf", "front", None),
            P("leaf", "front", None),
            P("leaf", "front", None),
        ),
        out_specs=P(None, "leaf", "front", None),
        check_vma=False,
    )
```

```python
import jax
import jax.numpy as jnp
import numpy as np
from jax import lax
from jax.sharding import PartitionSpec as P

BLK = 128
WIN = 24
PIECE = 40
LO = PIECE - WIN


def body(forcing, live, lower_inv, lower_upd, upper_inv, upper_upd):
    n_leaf = lax.axis_size("leaf")
    n_front = lax.axis_size("front")
    n_z = n_leaf // 2
    half = n_z // 2
    sep_dev, n_rhs = forcing.shape[1:]
    w0, w1 = sep_dev, sep_dev // 2
    n_plane = 2 * n_front
    height = n_front * WIN
    tail = w1 % n_rhs
    head = w1 - tail
    bf, f32, i32, u32 = jnp.bfloat16, jnp.float32, jnp.int32, jnp.uint32
    leaf_id = lax.axis_index("leaf").astype(u32)
    front_id = lax.axis_index("front").astype(u32)
    z, core = leaf_id // 2, leaf_id % 2
    node, z8 = z // half, z % half

    shift = half - 2
    turn = shift // 2
    fronts = [(k + shift) % n_front for k in range(n_front)]
    planes = [(k + shift) % n_z for k in range(n_z)]
    halves = [(k + turn) % half for k in range(half)]
    plane = [[(2 * k + c) * n_front + f for c in (1, 0) for f in fronts] for k in range(n_z)]
    z_all = [[2 * k + c for k in planes] for c in range(2)]
    z_half = [[2 * (h * half + k) + c for k in halves] for h in range(2) for c in range(2)]
    mid = half // 2
    middle_first = [mid] + [k for k in range(half) if k != mid]
    z_last = [[2 * (h * half + k) + c for k in middle_first] for h in range(2) for c in range(2)]
    swap = [(k, k ^ 1) for k in range(n_leaf)]

    def a2a_plane(v):
        return lax.all_to_all(v, ("leaf", "front"), 0, 0, axis_index_groups=plane)

    def a2a_leaf(v, groups):
        return lax.all_to_all(v, "leaf", 0, 0, axis_index_groups=groups)

    def place(k):
        return jnp.where(k == mid, u32(0), jnp.where(k < mid, k + 1, k))

    def spread(v, n):
        return jnp.broadcast_to(v[None], (n,) + v.shape)

    def by_core(even, odd):
        v = jnp.stack([odd, even])
        return jnp.broadcast_to(v[:, None], (2, n_front) + v.shape[1:]).reshape((n_plane,) + v.shape[1:])

    def cut(v):
        v = v.reshape(n_front, PIECE, v.shape[-1])
        return jnp.concatenate([v[:, :WIN], v[:, LO:]], 0)

    def join(v):
        low, high = v[:n_front], v[n_front:, WIN - LO :]
        return jnp.concatenate([low, high], 1).reshape(n_front * PIECE, v.shape[-1])

    def join_second(v):
        low, high = v[:n_front, :LO], v[n_front:]
        return jnp.concatenate([low, high], 1).reshape(n_front * PIECE, v.shape[-1])

    def lift(a, low):
        blank = jnp.zeros(a.shape[:-2] + (LO, n_rhs), a.dtype)
        first = jnp.concatenate([a, blank], -2)
        return jnp.where(low, first, jnp.concatenate([a[..., WIN - LO :, :], blank, blank[..., : WIN - LO, :]], -2))

    def lift_second(b, low):
        blank = jnp.zeros(b.shape[:-2] + (LO, n_rhs), b.dtype)
        first = jnp.concatenate([blank, blank[..., : WIN - LO, :], b[..., :LO, :]], -2)
        return jnp.where(low, first, jnp.concatenate([blank, b], -2))

    def pack(a, b, low):
        first = jnp.concatenate([a, b[..., :LO, :]], -2)
        return jnp.where(low, first, jnp.concatenate([a[..., WIN - LO :, :], b], -2))

    def unpack(v, low):
        return jnp.where(low, v[..., :WIN, :], jnp.concatenate([v[..., : WIN - LO, :], v[..., :LO, :]], -2))

    def unpack_second(v, low):
        first = jnp.concatenate([v[..., WIN:, :], v[..., LO:WIN, :]], -2)
        return jnp.where(low, first, v[..., LO:, :])

    def fold(v):
        return v[:n_front].astype(f32) + v[n_front:].astype(f32)

    def total(v):
        return jnp.sum(v.astype(f32), 0)

    def pick(v, k, n):
        return lax.dynamic_slice(v, (k,) + (np.uint32(0),) * (v.ndim - 1), (n,) + v.shape[1:])

    def masked(v, keep):
        return jnp.where(keep[..., None], v, 0.0).astype(bf)

    def dot(a, b):
        return jnp.dot(a, b, preferred_element_type=f32)

    def dot_pair(mat, first, last, v):
        m = mat.reshape(2, height, mat.shape[-1])[:, :, first:last]
        return lax.dot_general(m, v, (((0, 2), (0, 1)), ((), ())), preferred_element_type=f32)

    live_a, live_b, live_root = (live[k].reshape(()) * BLK for k in ((0, slice(0, 1)), (0, slice(1, 2)), (1, slice(0, 1))))
    live_node = jnp.where(node == 0, live_a, live_b)
    here = ((front_id + (n_front - shift)) % n_front * PIECE + (1 - core) * LO).astype(i32)
    at_out = (front_id * sep_dev + (core * half + place(z8)) * PIECE).astype(i32)
    kind = lax.iota(i32, 8)
    count = jnp.where(kind == 2, live_a, jnp.where(kind == 3, live_b, jnp.where((kind < 4) | (kind > 6), live_node, live_root)))
    block = jnp.where((kind > 1) & (kind < 5), z.astype(i32), 2 * z8.astype(i32) + ((kind == 1) | (kind == 6)).astype(i32))
    begin = jnp.where(kind == 7, at_out, here + block * sep_dev)
    keep = lax.broadcasted_iota(i32, (8, PIECE), 1) < (count - begin)[:, None]
    keep = tuple(keep[k, :WIN] for k in range(7)) + (keep[7],)
    scalars = (keep, core, 1 - core, (2 * z8 + (n_z - shift)) % n_z, place(front_id // 2), core == front_id % 2, core == 1)

    got = a2a_plane(cut(forcing[0]))
    uinv1 = cut(upper_inv[0, :, w0:])
    extra = jnp.concatenate([cut(lower_inv[0, :, w0:]), uinv1[:, :, head:]], 2)
    got, extra, uinv1, scalars = lax.optimization_barrier((got, extra, uinv1[:, :, :head], scalars))
    keep, core, other_core, two_z8, source, mine, low = scalars

    pair = fold(got).astype(bf).reshape(half, 2, WIN, n_rhs)
    pair = pack(pair[:, 0], pair[:, 1], low)
    r0 = total(a2a_leaf(pair, z_half))
    rm0 = by_core(masked(unpack(r0, low), keep[0]), masked(unpack_second(r0, low), keep[1]))
    moved = a2a_plane(jnp.concatenate([rm0, extra], 2))
    rm0 = moved[:, :, :n_rhs]
    rm0 = jnp.where(low, join_second(rm0), join(rm0))

    c_part = dot(lower_upd[0], rm0).astype(bf).reshape(n_front, PIECE, n_rhs)
    y_part = dot(lower_inv[0, :, :w0], rm0).astype(bf).reshape(n_front, PIECE, n_rhs)
    parts = jnp.stack(
        [
            jnp.concatenate([c_part[:, :WIN], y_part[:, :LO]], 1),
            jnp.concatenate([c_part[:, WIN:], y_part[:, LO:]], 1),
        ]
    )
    parts = fold(a2a_plane(parts.reshape(n_plane, PIECE, n_rhs))).astype(bf)

    got = a2a_leaf(parts, z_all)
    edge = half - shift
    sum_a, sum_b = total(got[:edge]) + total(got[edge + half :]), total(got[edge : edge + half])
    r1 = masked(-unpack(sum_a + sum_b, low), keep[4])
    y0_a, y0_b = masked(unpack_second(sum_a, low), keep[2]), masked(unpack_second(sum_b, low), keep[3])
    y0 = jnp.concatenate([spread(y0_a, edge), spread(y0_b, half), spread(y0_a, shift)], 0)
    r1, y0 = lax.optimization_barrier((spread(r1, n_plane), lift_second(y0, low)))
    r1 = join(a2a_plane(r1))

    blank = jnp.zeros((2, n_rhs - tail, n_rhs), bf)
    r1 = r1.reshape(2, w1, n_rhs)[::-1]
    y1 = dot_pair(moved, n_rhs, n_rhs + w1 + tail, jnp.concatenate([r1, blank], 1))
    got = a2a_leaf(lift(y1.astype(bf).reshape(n_front, WIN, n_rhs), low) + y0, z_all)
    y1 = masked(unpack(total(got), low), keep[4])
    y0 = unpack_second(lax.optimization_barrier(pick(got, two_z8, 2)), low)
    got = a2a_plane(jnp.concatenate([spread(y1, n_plane), by_core(y0[0], y0[1]), uinv1], 2))
    y1 = join(got[:, :, :n_rhs])
    y0 = join_second(got[:, :, n_rhs : 2 * n_rhs])

    y1 = y1.reshape(2, w1, n_rhs)[::-1]
    x1 = dot_pair(got, 2 * n_rhs, 2 * n_rhs + head, y1[:, :head])
    x1 = x1 + dot_pair(moved, n_rhs + head, n_rhs + head + n_rhs, jnp.concatenate([blank, y1[:, head:]], 1))
    x1 = x1.astype(bf).reshape(half, 2, WIN, n_rhs)
    x1 = pack(x1[:, 0], x1[:, 1], low)
    x1, y0 = lax.optimization_barrier((jnp.concatenate([x1[turn:], x1, x1[:turn]], 0), y0))
    x1, y0 = lax.optimization_barrier((total(a2a_leaf(x1, z_all)), y0))
    x1 = by_core(masked(unpack(x1, low), keep[5]), masked(unpack_second(x1, low), keep[6]))
    x1, term = lax.optimization_barrier((x1, dot(upper_inv[0, :, :w0], y0)))
    x1 = a2a_plane(x1)
    x1 = jnp.where(low, join_second(x1), join(x1))

    term = (term - dot(upper_upd[0], x1)).reshape(2, half, PIECE, n_rhs)
    x1 = x1.reshape(2, half, PIECE, n_rhs)
    away = jnp.concatenate([pick(term, other_core, 1)[0].astype(bf), pick(x1, other_core, 1)[0]], 1)
    away = lax.ppermute(away, "leaf", swap)
    term = (pick(term, core, 1)[0] + away[:, :PIECE].astype(f32)).astype(bf)
    own = jnp.where(mine, pick(x1, core, 1)[0], away[:, PIECE:])
    got = a2a_leaf(jnp.concatenate([term, own], 1), z_last)

    x0 = masked(total(got[:, :PIECE]), keep[7])
    x1 = pick(got[:, PIECE:], source, 1)[0]
    both = a2a_leaf(spread(jnp.stack([x0, x1]), half), z_last)
    both = jnp.swapaxes(both, 0, 1).reshape(2, half * PIECE, n_rhs)
    other = lax.ppermute(both, "leaf", swap)
    both = jnp.where(core == 0, jnp.concatenate([both, other], 1), jnp.concatenate([other, both], 1))
    return both[:, None]


def solution(mesh):
    return jax.shard_map(
        body,
        mesh=mesh,
        in_specs=(
            P("leaf", "front", None),
            P(),
            P("leaf", "front", None),
            P("leaf", "front", None),
            P("leaf", "front", None),
            P("leaf", "front", None),
        ),
        out_specs=P(None, "leaf", "front", None),
        check_vma=False,
    )
```

```python
import jax
import jax.numpy as jnp
import numpy as np
from jax import lax
from jax.experimental.layout import Layout, with_layout_constraint
from jax.sharding import PartitionSpec as P

BLK = 128
WIN = 24
PIECE = 40
LO = PIECE - WIN


def body(forcing, live, lower_inv, lower_upd, upper_inv, upper_upd):
    n_leaf = lax.axis_size("leaf")
    n_front = lax.axis_size("front")
    n_z = n_leaf // 2
    half = n_z // 2
    sep_dev, n_rhs = forcing.shape[1:]
    w0, w1 = sep_dev, sep_dev // 2
    n_plane = 2 * n_front
    height = n_front * WIN
    tail = w1 % n_rhs
    head = w1 - tail
    bf, f32, i32, u32 = jnp.bfloat16, jnp.float32, jnp.int32, jnp.uint32
    leaf_id = lax.axis_index("leaf").astype(u32)
    front_id = lax.axis_index("front").astype(u32)
    z, core = leaf_id // 2, leaf_id % 2
    node, z8 = z // half, z % half

    shift = half - 2
    turn = shift // 2
    fronts = [(k + shift) % n_front for k in range(n_front)]
    planes = [(k + shift) % n_z for k in range(n_z)]
    halves = [(k + turn) % half for k in range(half)]
    plane = [[(2 * k + c) * n_front + f for c in (1, 0) for f in fronts] for k in range(n_z)]
    z_all = [[2 * k + c for k in planes] for c in range(2)]
    z_half = [[2 * (h * half + k) + c for k in halves] for h in range(2) for c in range(2)]
    mid = half // 2
    middle_first = [mid] + [k for k in range(half) if k != mid]
    z_last = [[2 * (h * half + k) + c for k in middle_first] for h in range(2) for c in range(2)]
    swap = [(k, k ^ 1) for k in range(n_leaf)]

    def a2a_plane(v):
        return lax.all_to_all(v, ("leaf", "front"), 0, 0, axis_index_groups=plane)

    def a2a_leaf(v, groups):
        return lax.all_to_all(v, "leaf", 0, 0, axis_index_groups=groups)

    def place(k):
        return jnp.where(k == mid, u32(0), jnp.where(k < mid, k + 1, k))

    def spread(v, n):
        return jnp.broadcast_to(v[None], (n,) + v.shape)

    def by_core(even, odd):
        v = jnp.stack([odd, even])
        return jnp.broadcast_to(v[:, None], (2, n_front) + v.shape[1:]).reshape((n_plane,) + v.shape[1:])

    def cut(v):
        v = v.reshape(n_front, PIECE, v.shape[-1])
        return jnp.concatenate([v[:, :WIN], v[:, LO:]], 0)

    def join(v):
        low, high = v[:n_front], v[n_front:, WIN - LO :]
        return jnp.concatenate([low, high], 1).reshape(n_front * PIECE, v.shape[-1])

    def join_second(v):
        low, high = v[:n_front, :LO], v[n_front:]
        return jnp.concatenate([low, high], 1).reshape(n_front * PIECE, v.shape[-1])

    def lift(a, low):
        blank = jnp.zeros(a.shape[:-2] + (LO, n_rhs), a.dtype)
        first = jnp.concatenate([a, blank], -2)
        return jnp.where(low, first, jnp.concatenate([a[..., WIN - LO :, :], blank, blank[..., : WIN - LO, :]], -2))

    def lift_second(b, low):
        blank = jnp.zeros(b.shape[:-2] + (LO, n_rhs), b.dtype)
        first = jnp.concatenate([blank, blank[..., : WIN - LO, :], b[..., :LO, :]], -2)
        return jnp.where(low, first, jnp.concatenate([blank, b], -2))

    def pack(a, b, low):
        first = jnp.concatenate([a, b[..., :LO, :]], -2)
        return jnp.where(low, first, jnp.concatenate([a[..., WIN - LO :, :], b], -2))

    def unpack(v, low):
        return jnp.where(low, v[..., :WIN, :], jnp.concatenate([v[..., : WIN - LO, :], v[..., :LO, :]], -2))

    def unpack_second(v, low):
        first = jnp.concatenate([v[..., WIN:, :], v[..., LO:WIN, :]], -2)
        return jnp.where(low, first, v[..., LO:, :])

    def fold(v):
        return v[:n_front].astype(f32) + v[n_front:].astype(f32)

    def total(v):
        return jnp.sum(v.astype(f32), 0)

    def pick(v, k, n):
        return lax.dynamic_slice(v, (k,) + (np.uint32(0),) * (v.ndim - 1), (n,) + v.shape[1:])

    def masked(v, keep):
        return jnp.where(keep[..., None], v, 0.0).astype(bf)

    def dot(a, b):
        return with_layout_constraint(jnp.dot(a, b, preferred_element_type=f32), Layout((0, 1)))

    def dot_pair(mat, first, last, v):
        m = mat.reshape(2, height, mat.shape[-1])[:, :, first:last]
        return lax.dot_general(m, v, (((0, 2), (0, 1)), ((), ())), preferred_element_type=f32)

    live_a, live_b, live_root = (live[k].reshape(()) * BLK for k in ((0, slice(0, 1)), (0, slice(1, 2)), (1, slice(0, 1))))
    live_node = jnp.where(node == 0, live_a, live_b)
    here = ((front_id + (n_front - shift)) % n_front * PIECE + (1 - core) * LO).astype(i32)
    at_out = (front_id * sep_dev + (core * half + place(z8)) * PIECE).astype(i32)
    kind = lax.iota(i32, 8)
    count = jnp.where(kind == 2, live_a, jnp.where(kind == 3, live_b, jnp.where((kind < 4) | (kind > 6), live_node, live_root)))
    block = jnp.where((kind > 1) & (kind < 5), z.astype(i32), 2 * z8.astype(i32) + ((kind == 1) | (kind == 6)).astype(i32))
    begin = jnp.where(kind == 7, at_out, here + block * sep_dev)
    keep = lax.broadcasted_iota(i32, (8, PIECE), 1) < (count - begin)[:, None]
    keep = tuple(keep[k, :WIN] for k in range(7)) + (keep[7],)
    scalars = (keep, core, 1 - core, (2 * z8 + (n_z - shift)) % n_z, place(front_id // 2), core == front_id % 2, core == 1)

    got = a2a_plane(cut(forcing[0]))
    uinv1 = cut(upper_inv[0, :, w0:])
    extra = jnp.concatenate([cut(lower_inv[0, :, w0:]), uinv1[:, :, head:]], 2)
    got, extra, uinv1, scalars = lax.optimization_barrier((got, extra, uinv1[:, :, :head], scalars))
    keep, core, other_core, two_z8, source, mine, low = scalars

    pair = fold(got).astype(bf).reshape(half, 2, WIN, n_rhs)
    pair = pack(pair[:, 0], pair[:, 1], low)
    r0 = total(a2a_leaf(pair, z_half))
    rm0 = by_core(masked(unpack(r0, low), keep[0]), masked(unpack_second(r0, low), keep[1]))
    moved = a2a_plane(jnp.concatenate([rm0, extra], 2))
    rm0 = moved[:, :, :n_rhs]
    rm0 = jnp.where(low, join_second(rm0), join(rm0))

    c_part = dot(lower_upd[0], rm0).astype(bf).reshape(n_front, PIECE, n_rhs)
    y_part = dot(lower_inv[0, :, :w0], rm0).astype(bf).reshape(n_front, PIECE, n_rhs)
    parts = jnp.stack(
        [
            jnp.concatenate([c_part[:, :WIN], y_part[:, :LO]], 1),
            jnp.concatenate([c_part[:, WIN:], y_part[:, LO:]], 1),
        ]
    )
    parts = fold(a2a_plane(parts.reshape(n_plane, PIECE, n_rhs))).astype(bf)

    got = a2a_leaf(parts, z_all)
    edge = half - shift
    sum_a, sum_b = total(got[:edge]) + total(got[edge + half :]), total(got[edge : edge + half])
    r1 = masked(-unpack(sum_a + sum_b, low), keep[4])
    y0_a, y0_b = masked(unpack_second(sum_a, low), keep[2]), masked(unpack_second(sum_b, low), keep[3])
    y0 = jnp.concatenate([spread(y0_a, edge), spread(y0_b, half), spread(y0_a, shift)], 0)
    r1, y0 = lax.optimization_barrier((spread(r1, n_plane), lift_second(y0, low)))
    r1 = join(a2a_plane(r1))

    blank = jnp.zeros((2, n_rhs - tail, n_rhs), bf)
    r1 = r1.reshape(2, w1, n_rhs)[::-1]
    y1 = dot_pair(moved, n_rhs, n_rhs + w1 + tail, jnp.concatenate([r1, blank], 1))
    got = a2a_leaf(lift(y1.astype(bf).reshape(n_front, WIN, n_rhs), low) + y0, z_all)
    y1 = masked(unpack(total(got), low), keep[4])
    y0 = unpack_second(lax.optimization_barrier(pick(got, two_z8, 2)), low)
    got = a2a_plane(jnp.concatenate([spread(y1, n_plane), by_core(y0[0], y0[1]), uinv1], 2))
    y1 = join(got[:, :, :n_rhs])
    y0 = join_second(got[:, :, n_rhs : 2 * n_rhs])

    y1 = y1.reshape(2, w1, n_rhs)[::-1]
    x1 = dot_pair(got, 2 * n_rhs, 2 * n_rhs + head, y1[:, :head])
    x1 = x1 + dot_pair(moved, n_rhs + head, n_rhs + head + n_rhs, jnp.concatenate([blank, y1[:, head:]], 1))
    x1 = x1.astype(bf).reshape(half, 2, WIN, n_rhs)
    x1 = pack(x1[:, 0], x1[:, 1], low)
    x1, y0 = lax.optimization_barrier((jnp.concatenate([x1[turn:], x1, x1[:turn]], 0), y0))
    x1, y0 = lax.optimization_barrier((total(a2a_leaf(x1, z_all)), y0))
    x1 = by_core(masked(unpack(x1, low), keep[5]), masked(unpack_second(x1, low), keep[6]))
    x1, term = lax.optimization_barrier((x1, dot(upper_inv[0, :, :w0], y0)))
    x1 = a2a_plane(x1)
    x1 = jnp.where(low, join_second(x1), join(x1))

    term = (term - dot(upper_upd[0], x1)).reshape(2, half, PIECE, n_rhs)
    x1 = x1.reshape(2, half, PIECE, n_rhs)
    away = jnp.concatenate([pick(term, other_core, 1)[0].astype(bf), pick(x1, other_core, 1)[0]], 1)
    away = lax.ppermute(away, "leaf", swap)
    term = (pick(term, core, 1)[0] + away[:, :PIECE].astype(f32)).astype(bf)
    own = jnp.where(mine, pick(x1, core, 1)[0], away[:, PIECE:])
    got = a2a_leaf(jnp.concatenate([term, own], 1), z_last)

    x0 = masked(total(got[:, :PIECE]), keep[7])
    x1 = pick(got[:, PIECE:], source, 1)[0]
    both = a2a_leaf(spread(jnp.stack([x0, x1]), half), z_last)
    both = jnp.swapaxes(both, 0, 1).reshape(2, half * PIECE, n_rhs)
    other = lax.ppermute(both, "leaf", swap)
    both = jnp.where(core == 0, jnp.concatenate([both, other], 1), jnp.concatenate([other, both], 1))
    return both[:, None]


def solution(mesh):
    return jax.shard_map(
        body,
        mesh=mesh,
        in_specs=(
            P("leaf", "front", None),
            P(),
            P("leaf", "front", None),
            P("leaf", "front", None),
            P("leaf", "front", None),
            P("leaf", "front", None),
        ),
        out_specs=P(None, "leaf", "front", None),
        check_vma=False,
    )
```

```python
import jax
import jax.numpy as jnp
import numpy as np
from jax import lax
from jax.sharding import PartitionSpec as P

BLK = 128
WIN = 24
PIECE = 40
LO = PIECE - WIN


def body(forcing, live, lower_inv, lower_upd, upper_inv, upper_upd):
    n_leaf = lax.axis_size("leaf")
    n_front = lax.axis_size("front")
    n_z = n_leaf // 2
    half = n_z // 2
    sep_dev, n_rhs = forcing.shape[1:]
    w0, w1 = sep_dev, sep_dev // 2
    n_plane = 2 * n_front
    height = n_front * WIN
    tail = w1 % n_rhs
    head = w1 - tail
    bf, f32, i32, u32 = jnp.bfloat16, jnp.float32, jnp.int32, jnp.uint32
    leaf_id = lax.axis_index("leaf").astype(u32)
    front_id = lax.axis_index("front").astype(u32)
    z, core = leaf_id // 2, leaf_id % 2
    node, z8 = z // half, z % half

    shift = half
    turn = shift // 2
    fronts = [(k + shift) % n_front for k in range(n_front)]
    planes = [(k + shift) % n_z for k in range(n_z)]
    halves = [(k + turn) % half for k in range(half)]
    plane = [[(2 * k + c) * n_front + f for c in (1, 0) for f in fronts] for k in range(n_z)]
    z_all = [[2 * k + c for k in planes] for c in range(2)]
    z_half = [[2 * (h * half + k) + c for k in halves] for h in range(2) for c in range(2)]
    mid = half // 2
    middle_first = [mid] + [k for k in range(half) if k != mid]
    z_last = [[2 * (h * half + k) + c for k in middle_first] for h in range(2) for c in range(2)]
    swap = [(k, k ^ 1) for k in range(n_leaf)]

    def a2a_plane(v):
        return lax.all_to_all(v, ("leaf", "front"), 0, 0, axis_index_groups=plane)

    def a2a_leaf(v, groups):
        return lax.all_to_all(v, "leaf", 0, 0, axis_index_groups=groups)

    def place(k):
        return jnp.where(k == mid, u32(0), jnp.where(k < mid, k + 1, k))

    def spread(v, n):
        return jnp.broadcast_to(v[None], (n,) + v.shape)

    def by_core(even, odd):
        v = jnp.stack([odd, even])
        return jnp.broadcast_to(v[:, None], (2, n_front) + v.shape[1:]).reshape((n_plane,) + v.shape[1:])

    def cut(v):
        v = v.reshape(n_front, PIECE, v.shape[-1])
        return jnp.concatenate([v[:, :WIN], v[:, LO:]], 0)

    def join(v):
        low, high = v[:n_front], v[n_front:, WIN - LO :]
        return jnp.concatenate([low, high], 1).reshape(n_front * PIECE, v.shape[-1])

    def join_second(v):
        low, high = v[:n_front, :LO], v[n_front:]
        return jnp.concatenate([low, high], 1).reshape(n_front * PIECE, v.shape[-1])

    def lift(a, low):
        blank = jnp.zeros(a.shape[:-2] + (LO, n_rhs), a.dtype)
        first = jnp.concatenate([a, blank], -2)
        return jnp.where(low, first, jnp.concatenate([a[..., WIN - LO :, :], blank, blank[..., : WIN - LO, :]], -2))

    def lift_second(b, low):
        blank = jnp.zeros(b.shape[:-2] + (LO, n_rhs), b.dtype)
        first = jnp.concatenate([blank, blank[..., : WIN - LO, :], b[..., :LO, :]], -2)
        return jnp.where(low, first, jnp.concatenate([blank, b], -2))

    def pack(a, b, low):
        first = jnp.concatenate([a, b[..., :LO, :]], -2)
        return jnp.where(low, first, jnp.concatenate([a[..., WIN - LO :, :], b], -2))

    def unpack(v, low):
        return jnp.where(low, v[..., :WIN, :], jnp.concatenate([v[..., : WIN - LO, :], v[..., :LO, :]], -2))

    def unpack_second(v, low):
        first = jnp.concatenate([v[..., WIN:, :], v[..., LO:WIN, :]], -2)
        return jnp.where(low, first, v[..., LO:, :])

    def fold(v):
        return v[:n_front].astype(f32) + v[n_front:].astype(f32)

    def total(v):
        return jnp.sum(v.astype(f32), 0)

    def pick(v, k, n):
        return lax.dynamic_slice(v, (k,) + (np.uint32(0),) * (v.ndim - 1), (n,) + v.shape[1:])

    def masked(v, keep):
        return jnp.where(keep[..., None], v, 0.0).astype(bf)

    def dot(a, b):
        return jnp.dot(a, b, preferred_element_type=f32)

    def dot_pair(mat, first, last, v):
        m = mat.reshape(2, height, mat.shape[-1])[:, :, first:last]
        return lax.dot_general(m, v, (((0, 2), (0, 1)), ((), ())), preferred_element_type=f32)

    live_a, live_b, live_root = (live[k].reshape(()) * BLK for k in ((0, slice(0, 1)), (0, slice(1, 2)), (1, slice(0, 1))))
    live_node = jnp.where(node == 0, live_a, live_b)
    here = ((front_id + (n_front - shift)) % n_front * PIECE + (1 - core) * LO).astype(i32)
    at_out = (front_id * sep_dev + (core * half + place(z8)) * PIECE).astype(i32)
    kind = lax.iota(i32, 8)
    count = jnp.where(kind == 2, live_a, jnp.where(kind == 3, live_b, jnp.where((kind < 4) | (kind > 6), live_node, live_root)))
    block = jnp.where((kind > 1) & (kind < 5), z.astype(i32), 2 * z8.astype(i32) + ((kind == 1) | (kind == 6)).astype(i32))
    begin = jnp.where(kind == 7, at_out, here + block * sep_dev)
    keep = lax.broadcasted_iota(i32, (8, PIECE), 1) < (count - begin)[:, None]
    keep = tuple(keep[k, :WIN] for k in range(7)) + (keep[7],)
    scalars = (keep, core, 1 - core, (2 * z8 + (n_z - shift)) % n_z, place(front_id // 2), core == front_id % 2, core == 1)

    got = a2a_plane(cut(forcing[0]))
    uinv1 = cut(upper_inv[0, :, w0:])
    extra = jnp.concatenate([cut(lower_inv[0, :, w0:]), uinv1[:, :, head:]], 2)
    got, extra, uinv1, scalars = lax.optimization_barrier((got, extra, uinv1[:, :, :head], scalars))
    keep, core, other_core, two_z8, source, mine, low = scalars

    pair = fold(got).astype(bf).reshape(half, 2, WIN, n_rhs)
    pair = pack(pair[:, 0], pair[:, 1], low)
    r0 = total(a2a_leaf(pair, z_half))
    rm0 = by_core(masked(unpack(r0, low), keep[0]), masked(unpack_second(r0, low), keep[1]))
    moved = a2a_plane(jnp.concatenate([rm0, extra], 2))
    rm0 = moved[:, :, :n_rhs]
    rm0 = jnp.where(low, join_second(rm0), join(rm0))

    c_part = dot(lower_upd[0], rm0).astype(bf).reshape(n_front, PIECE, n_rhs)
    y_part = dot(lower_inv[0, :, :w0], rm0).astype(bf).reshape(n_front, PIECE, n_rhs)
    parts = jnp.stack(
        [
            jnp.concatenate([c_part[:, :WIN], y_part[:, :LO]], 1),
            jnp.concatenate([c_part[:, WIN:], y_part[:, LO:]], 1),
        ]
    )
    parts = fold(a2a_plane(parts.reshape(n_plane, PIECE, n_rhs))).astype(bf)

    got = a2a_leaf(parts, z_all)
    edge = half - shift
    sum_a, sum_b = total(got[:edge]) + total(got[edge + half :]), total(got[edge : edge + half])
    r1 = masked(-unpack(sum_a + sum_b, low), keep[4])
    y0_a, y0_b = masked(unpack_second(sum_a, low), keep[2]), masked(unpack_second(sum_b, low), keep[3])
    y0 = jnp.concatenate([spread(y0_a, edge), spread(y0_b, half), spread(y0_a, shift)], 0)
    r1, y0 = lax.optimization_barrier((spread(r1, n_plane), lift_second(y0, low)))
    r1 = join(a2a_plane(r1))

    blank = jnp.zeros((2, n_rhs - tail, n_rhs), bf)
    r1 = r1.reshape(2, w1, n_rhs)[::-1]
    y1 = dot_pair(moved, n_rhs, n_rhs + w1 + tail, jnp.concatenate([r1, blank], 1))
    got = a2a_leaf(lift(y1.astype(bf).reshape(n_front, WIN, n_rhs), low) + y0, z_all)
    y1 = masked(unpack(total(got), low), keep[4])
    y0 = unpack_second(lax.optimization_barrier(pick(got, two_z8, 2)), low)
    got = a2a_plane(jnp.concatenate([spread(y1, n_plane), by_core(y0[0], y0[1]), uinv1], 2))
    y1 = join(got[:, :, :n_rhs])
    y0 = join_second(got[:, :, n_rhs : 2 * n_rhs])

    y1 = y1.reshape(2, w1, n_rhs)[::-1]
    x1 = dot_pair(got, 2 * n_rhs, 2 * n_rhs + head, y1[:, :head])
    x1 = x1 + dot_pair(moved, n_rhs + head, n_rhs + head + n_rhs, jnp.concatenate([blank, y1[:, head:]], 1))
    x1 = x1.astype(bf).reshape(half, 2, WIN, n_rhs)
    x1 = pack(x1[:, 0], x1[:, 1], low)
    x1, y0 = lax.optimization_barrier((jnp.concatenate([x1[turn:], x1, x1[:turn]], 0), y0))
    x1, y0 = lax.optimization_barrier((total(a2a_leaf(x1, z_all)), y0))
    x1 = by_core(masked(unpack(x1, low), keep[5]), masked(unpack_second(x1, low), keep[6]))
    x1, term = lax.optimization_barrier((x1, dot(upper_inv[0, :, :w0], y0)))
    x1 = a2a_plane(x1)
    x1 = jnp.where(low, join_second(x1), join(x1))

    term = (term - dot(upper_upd[0], x1)).reshape(2, half, PIECE, n_rhs)
    x1 = x1.reshape(2, half, PIECE, n_rhs)
    away = jnp.concatenate([pick(term, other_core, 1)[0].astype(bf), pick(x1, other_core, 1)[0]], 1)
    away = lax.ppermute(away, "leaf", swap)
    term = (pick(term, core, 1)[0] + away[:, :PIECE].astype(f32)).astype(bf)
    own = jnp.where(mine, pick(x1, core, 1)[0], away[:, PIECE:])
    got = a2a_leaf(jnp.concatenate([term, own], 1), z_last)

    x0 = masked(total(got[:, :PIECE]), keep[7])
    x1 = pick(got[:, PIECE:], source, 1)[0]
    both = a2a_leaf(spread(jnp.stack([x0, x1]), half), z_last)
    both = jnp.swapaxes(both, 0, 1).reshape(2, half * PIECE, n_rhs)
    other = lax.ppermute(both, "leaf", swap)
    both = jnp.where(core == 0, jnp.concatenate([both, other], 1), jnp.concatenate([other, both], 1))
    return both[:, None]


def solution(mesh):
    return jax.shard_map(
        body,
        mesh=mesh,
        in_specs=(
            P("leaf", "front", None),
            P(),
            P("leaf", "front", None),
            P("leaf", "front", None),
            P("leaf", "front", None),
            P("leaf", "front", None),
        ),
        out_specs=P(None, "leaf", "front", None),
        check_vma=False,
    )
```
